32 devices in a mesh: groups: 2 (over y), brick: 4 (over z), ray: 4 (over x, core).
Axes of the slice: x: 2, y: 2, z: 4, core: 2. Of those that a mesh axis runs over, the one named last changes fastest.
Arguments:
- samples_in: bfloat16 [2048, 4, 32, 128], P(('groups', 'ray'), 'brick'), parts along dimension 0, may hold values from -6 to 6
- sample_count: int32 [2048, 4], P(('groups', 'ray'), 'brick'), parts along dimension 0, may hold values from 0 to 32, as said below
- step_length: float32 [2048], P(('groups', 'ray')), parts along dimension 0, may hold values from 0.001 to 0.008
- view_flip: int32 [2048], P(('groups', 'ray')), parts along dimension 0, may hold values 0 or 1
- pixel_grad: float32 [64, 2048], P(None, ('groups', 'ray')), parts along dimension 1, may hold values from -6 to 6
- w_first: bfloat16 [4, 128, 128], P('brick'), may hold values from -0.5 to 0.5
- w_second: bfloat16 [4, 128, 128], P('brick'), may hold values from -0.5 to 0.5
- w_feature: bfloat16 [4, 128, 64], P('brick'), may hold values from -0.5 to 0.5
- w_density: bfloat16 [4, 128], P('brick'), may hold values from -0.5 to 0.5
Outputs:
- grad_samples: bfloat16 [2048, 4, 32, 128], P(('groups', 'ray'), 'brick'), parts along dimension 0
- grad_first: float32 [8, 128, 128], P(('groups', 'brick'), 'ray'), parts along dimension 0
- grad_second: float32 [8, 128, 128], P(('groups', 'brick'), 'ray'), parts along dimension 0
- grad_feature: float32 [8, 128, 64], P(('groups', 'brick'), 'ray'), parts along dimension 0
- grad_density: float32 [8, 128], P(('groups', 'brick'), 'ray'), parts along dimension 0
The draws below stay inside these ranges and needn't reach their ends.
There are 2 independent parts, one for each index of `groups`. The reference program is written for one: setup_inputs(seed, part) draws one part's arguments, and reference() takes and returns one part's arrays. A program takes and returns all parts, laid end to end along the dimension named above; an argument that names none is the same for every part. Nothing has to cross between parts.
Inputs may be any that keep to these rules, and one draw needn't show every extreme that they name: A ray's samples inside a brick are the first sample_count of its block.
All inputs are finite; a program needn't handle non-finite values. No bound on the sum of `view_flip` on one device may be relied on, other than what follows from the above.
Results may differ from the reference program's by a relative error of at most 0.0045.
The reference program's roundings to bfloat16 on the way (of `hidden_one`, `hidden_two`, `logit_grad`, `feature_grad`, `pre_two_grad` and `pre_one_grad`) count: a program that leaves them out, or rounds other values in their place, can miss the bound.
Values sent between devices are 32-bit elements; how exact they have to be, the bound alone decides.
A program may use at most 64 MiB of HBM per device.

```python
import math
import jax
import jax.numpy as jnp
from jax import lax

WIDTH = 128
FEAT = 64
S_BLK = 32
RAYS = 1024
BRICKS = 4


def draw_sample_count(key, part):
    counts = jax.random.randint(key, (RAYS, BRICKS), 0, S_BLK + 1, dtype=jnp.int32)
    counts = counts.at[0, 0].set(S_BLK)
    counts = counts.at[0, 1].set(0)
    return counts


def with_ends(values, stream_key, least, high):
    longest = values.shape.index(max(values.shape))
    spots = []
    for shift in (0, 1):
        where = [jax.random.randint(jax.random.fold_in(stream_key, axis), (), 0, length) for axis, length in enumerate(values.shape)]
        where[longest] = (where[longest] + shift) % values.shape[longest]
        spots.append(tuple(where))
    return values.at[spots[0]].set(least).at[spots[1]].set(high)


def block_scale(own_key, extent, pieces, low, largest):
    def one(dim, blocks):
        steps = jax.random.uniform(jax.random.fold_in(jax.random.fold_in(own_key, 6), dim), (blocks,), jnp.float32, low / len(pieces), largest / len(pieces))
        return jnp.repeat(jnp.exp(steps), extent[dim] // blocks).reshape((-1,) + (1,) * (len(extent) - dim - 1))

    gain = one(*pieces[0])
    for cut in pieces[1:]:
        gain = gain * one(*cut)
    return gain


def gaussian(stream_key, shape, deviation, reach, split=(), kind=jnp.bfloat16):
    entries = jax.random.normal(stream_key, shape, jnp.float32) * deviation
    if len(split) > 0:
        entries = block_scale(stream_key, shape, split, -0.22, 0.18) * entries
    return jnp.clip(entries, min=-reach, max=reach).astype(kind)


def setup_inputs(seed: int = 0, part: int = 0) -> dict:
    key_list = jax.random.split(jax.random.key(seed), 10)
    part_splits = jax.random.split(jax.random.fold_in(key_list[9], part), 10)
    return {
        "samples_in": gaussian(part_splits[0], (RAYS, BRICKS, S_BLK, WIDTH), 1.0, 6.0, ((0, 4), (1, 4))),
        "sample_count": draw_sample_count(jax.random.fold_in(jax.random.fold_in(key_list[9], part), 71), part),
        "step_length": jnp.clip(jnp.exp(math.log(0.008) - 2.0794415 * jax.random.uniform(part_splits[2], (RAYS,), jnp.float32) ** block_scale(part_splits[2], (RAYS,), ((0, 4),), -0.2, 0.2)), 0.001, 0.008),
        "view_flip": with_ends((jax.random.randint(part_splits[3], (RAYS,), 0, 2) < 1).astype(jnp.int32), jax.random.fold_in(part_splits[3], 1), 0, 1),
        "pixel_grad": gaussian(part_splits[4], (FEAT, RAYS), 1.0, 6.0, ((1, 4),), jnp.float32),
        "w_first": gaussian(key_list[5], (BRICKS, WIDTH, WIDTH), WIDTH ** -0.5, 0.5, ((0, 4),)),
        "w_second": gaussian(key_list[6], (BRICKS, WIDTH, WIDTH), WIDTH ** -0.5, 0.5, ((0, 4),)),
        "w_feature": gaussian(key_list[7], (BRICKS, WIDTH, FEAT), WIDTH ** -0.5, 0.5, ((0, 4),)),
        "w_density": gaussian(key_list[8], (BRICKS, WIDTH), WIDTH ** -0.5, 0.5, ((0, 4),)),
    }


LOSS_SCALE = 1024.0


def silu_slope(pre_act):
    sigmoid_pre = jax.nn.sigmoid(pre_act)
    return sigmoid_pre * (1.0 + pre_act * (1.0 - sigmoid_pre))


def contract_rows(left, right):
    return lax.dot_general(left, right, (((0,), (0,)), ((), ())), preferred_element_type=jnp.float32)


def brick_forward(block, first_map, second_map, feature_map, density_map, counts, step_length):
    rays_here = block.shape[0]
    per_ray = block.shape[1]
    inputs = block.reshape(rays_here * per_ray, block.shape[2])
    pre_one = jnp.dot(inputs, first_map, preferred_element_type=jnp.float32)
    hidden_one = jax.nn.silu(pre_one).astype(jnp.bfloat16)
    pre_two = jnp.dot(hidden_one, second_map, preferred_element_type=jnp.float32)
    hidden_two = jax.nn.silu(pre_two).astype(jnp.bfloat16)
    features = jnp.dot(hidden_two, feature_map, preferred_element_type=jnp.float32)
    logits = jnp.dot(hidden_two, density_map, preferred_element_type=jnp.float32).reshape(rays_here, per_ray)
    is_valid = lax.broadcasted_iota(jnp.int32, (rays_here, per_ray), 1) < counts
    depth_step = jnp.where(is_valid, jax.nn.softplus(logits) * step_length[:, None], 0.0)
    depth_incl = jnp.cumsum(depth_step, axis=1)
    depth_excl = depth_incl - depth_step
    weights = jnp.exp(-depth_excl) * (-jnp.expm1(-depth_step))
    feat_rays = features.reshape(rays_here, per_ray, -1)
    brick_depth = depth_incl[:, -1]
    brick_color = jnp.einsum("rs,rsf->fr", weights, feat_rays, precision=lax.Precision.HIGHEST)
    return (inputs, pre_one, hidden_one, pre_two, hidden_two, feat_rays, logits, is_valid,
            depth_incl, weights, brick_depth, brick_color)


def brick_backward(state, second_map, first_map, feature_map, density_map, step_length, front_depth, behind_color, scaled):
    (inputs, pre_one, hidden_one, pre_two, hidden_two, feat_rays, logits, is_valid,
     depth_incl, weights, brick_depth, brick_color) = state
    rays_here = feat_rays.shape[0]
    per_ray = feat_rays.shape[1]
    through_front = jnp.exp(-front_depth)
    brick_grad = -through_front * jnp.exp(-brick_depth) * jnp.sum(scaled * behind_color, axis=0)
    own_grad = through_front[:, None] * jnp.einsum("rsf,fr->rs", feat_rays, scaled, precision=lax.Precision.HIGHEST)
    weighted = weights * own_grad
    later_sum = jnp.sum(weighted, axis=1, keepdims=True) - jnp.cumsum(weighted, axis=1)
    step_grad = jnp.exp(-depth_incl) * own_grad - later_sum + brick_grad[:, None]
    logit_grad = jnp.where(is_valid, step_grad * step_length[:, None] * jax.nn.sigmoid(logits), 0.0)
    logit_grad = logit_grad.astype(jnp.bfloat16).reshape(rays_here * per_ray)
    feature_grad = (through_front[:, None] * weights)[:, :, None] * jnp.transpose(scaled)[:, None, :]
    feature_grad = feature_grad.astype(jnp.bfloat16).reshape(rays_here * per_ray, -1)
    hidden_grad = lax.dot_general(feature_grad, feature_map, (((1,), (1,)), ((), ())), preferred_element_type=jnp.float32)
    hidden_grad = hidden_grad + logit_grad.astype(jnp.float32)[:, None] * density_map.astype(jnp.float32)[None, :]
    pre_two_grad = (hidden_grad * silu_slope(pre_two)).astype(jnp.bfloat16)
    hidden_one_grad = lax.dot_general(pre_two_grad, second_map, (((1,), (1,)), ((), ())), preferred_element_type=jnp.float32)
    pre_one_grad = (hidden_one_grad * silu_slope(pre_one)).astype(jnp.bfloat16)
    input_grad = lax.dot_general(pre_one_grad, first_map, (((1,), (1,)), ((), ())), preferred_element_type=jnp.float32)
    input_grad = input_grad.astype(jnp.bfloat16).reshape(rays_here, per_ray, -1)
    grad_one = contract_rows(inputs, pre_one_grad)
    grad_two = contract_rows(hidden_one, pre_two_grad)
    grad_three = contract_rows(hidden_two, feature_grad)
    grad_four = jnp.dot(logit_grad, hidden_two, preferred_element_type=jnp.float32)
    return input_grad, grad_one, grad_two, grad_three, grad_four


def reference(samples_in, sample_count, step_length, view_flip, pixel_grad, w_first, w_second, w_feature, w_density):
    blocks = jnp.moveaxis(samples_in, 1, 0)
    counts_t = jnp.transpose(sample_count)[:, :, None]

    def forward_one(items):
        state = brick_forward(items[0], items[1], items[2], items[3], items[4], items[5], step_length)
        return state[10], state[11]

    depths, colors = lax.map(forward_one, (blocks, w_first, w_second, w_feature, w_density, counts_t))
    cumulative = jnp.cumsum(depths, axis=0)
    lower_depth = cumulative - depths
    upper_depth = cumulative[-1][None, :] - cumulative
    brick_order = lax.broadcasted_iota(jnp.int32, (depths.shape[0], 1), 0)

    def behind_pair(index):
        through = cumulative[index]
        before = through - depths[index]
        after_gap = jnp.where(brick_order > index, cumulative - depths - through[None, :], 0.0)
        before_gap = jnp.where(brick_order < index, before[None, :] - cumulative, 0.0)
        upper_weight = jnp.where(brick_order > index, jnp.exp(-after_gap), 0.0)
        lower_weight = jnp.where(brick_order < index, jnp.exp(-before_gap), 0.0)
        upper_color = jnp.einsum("kr,kfr->fr", upper_weight, colors, precision=lax.Precision.HIGHEST)
        lower_color = jnp.einsum("kr,kfr->fr", lower_weight, colors, precision=lax.Precision.HIGHEST)
        return upper_color, lower_color

    upper_colors, lower_colors = lax.map(behind_pair, jnp.arange(depths.shape[0], dtype=jnp.int32))
    flipped = view_flip > 0
    front_depth = jnp.where(flipped[None, :], upper_depth, lower_depth)
    behind_color = jnp.where(flipped[None, None, :], lower_colors, upper_colors)
    scaled = LOSS_SCALE * pixel_grad

    def backward_one(items):
        state = brick_forward(items[0], items[1], items[2], items[3], items[4], items[5], step_length)
        return brick_backward(state, items[2], items[1], items[3], items[4], step_length, items[6], items[7], scaled)

    input_grads, grad_one, grad_two, grad_three, grad_four = lax.map(
        backward_one, (blocks, w_first, w_second, w_feature, w_density, counts_t, front_depth, behind_color))
    grad_samples = jnp.moveaxis(input_grads, 0, 1)
    return (grad_samples, grad_one / LOSS_SCALE, grad_two / LOSS_SCALE, grad_three / LOSS_SCALE, grad_four / LOSS_SCALE)
```

```python
import functools

import jax
import jax.numpy as jnp
from jax import lax
from jax.experimental import pallas as pl
from jax.experimental.pallas import tpu as pltpu
from jax.sharding import PartitionSpec as P

LOSS_SCALE = 1024.0
LANES = 256
UNROLL_FORWARD = 1
UNROLL_BACK = True
PIECES = 8
F32 = jnp.float32
BF16 = jnp.bfloat16
MESH = pl.DeviceIdType.MESH


def iota(shape, dim):
    return lax.broadcasted_iota(jnp.int32, shape, dim)


def split_two(v):
    hi = v.astype(BF16).astype(F32)
    return hi, v - hi


def dot_exact(v, m):
    rows = v.shape[0]
    hi, rest = split_two(v)
    mid, low = split_two(rest)
    out = jnp.dot(
        jnp.concatenate([hi, mid, low], axis=0).astype(BF16), m, preferred_element_type=F32
    )
    return out[:rows] + out[rows : 2 * rows] + out[2 * rows :]


def block_diag(w):
    z = jnp.zeros_like(w)
    return jnp.concatenate(
        [jnp.concatenate([w, z], axis=1), jnp.concatenate([z, w], axis=1)], axis=0
    )


def side(v, right):
    z = jnp.zeros_like(v)
    return jnp.concatenate([z, v] if right else [v, z], axis=1)


def silu_pair(half):
    t = jnp.tanh(half)
    a = 1.0 + t
    h = half * a
    slope = a + h * (1.0 - t)
    return h, slope


def kernel(
    n_brick,
    n_ray,
    per_ray,
    x_hbm,
    count_ref,
    step_ref,
    flip_ref,
    pg_ref,
    w1_ref,
    w2_ref,
    wf_ref,
    wd_ref,
    o_hbm,
    g1_ref,
    g2_ref,
    g3_ref,
    g4_ref,
    x_ref,
    o_ref,
    h1_ref,
    h2_ref,
    xt_ref,
    h1t_ref,
    h2t_ref,
    pre1_even,
    pre1_odd,
    pre2_even,
    pre2_odd,
    s1_ref,
    s2_ref,
    p1_ref,
    p2_ref,
    fg_ref,
    v_ref,
    sc_ref,
    q_ref,
    lg_ref,
    c_ref,
    w1f,
    w2f,
    w1b,
    w2b,
    wfb,
    acc,
    ex_ref,
    red_ref,
    in_sem,
    out_sem,
    ex_send,
    ex_recv,
    red_send,
    red_recv,
):
    rows, width = x_ref.shape
    rays = pg_ref.shape[1]
    feat = pg_ref.shape[0]
    group = LANES // per_ray
    tiles = rows // LANES
    pairs = tiles // 2
    span = 2 * LANES

    x_copy = pltpu.make_async_copy(x_hbm, x_ref, in_sem)
    x_copy.start()

    def out_copy(p):
        at = pl.ds(pl.multiple_of(p * span, span), span)
        return pltpu.make_async_copy(o_ref.at[at], o_hbm.at[at], out_sem.at[p])

    my_brick = lax.axis_index("brick")
    my_ray = lax.axis_index("ray")
    barrier = pltpu.get_barrier_semaphore()
    for d in range(1, n_brick):
        pl.semaphore_signal(
            barrier, inc=1, device_id={"brick": lax.rem(my_brick + d, n_brick)}, device_id_type=MESH
        )
    for d in range(1, n_ray):
        pl.semaphore_signal(
            barrier, inc=1, device_id={"ray": lax.rem(my_ray + d, n_ray)}, device_id_type=MESH
        )

    w1 = w1_ref[0].astype(F32)
    w2 = w2_ref[0].astype(F32)
    wf = wf_ref[0].astype(F32)
    wd = wd_ref[...].astype(F32)
    w1f[...] = block_diag(w1 * 0.5).astype(BF16)
    w2f[...] = block_diag(w2 * 0.5).astype(BF16)
    wide = jnp.concatenate(
        [wf, wd, jnp.zeros((width - feat - 1, width), F32)], axis=0
    )
    wfb[...] = block_diag(wide * 0.5).astype(BF16)
    scaled = jnp.concatenate(
        [LOSS_SCALE * pg_ref[...], jnp.zeros((width - feat, rays), F32)], axis=0
    ).T
    sc_ref[...] = scaled
    v_ref[...] = dot_exact(scaled, wide.astype(BF16))
    acc[...] = jnp.zeros_like(acc)
    group_mask = (iota((group, LANES), 0) == iota((group, LANES), 1) // per_ray).astype(F32)
    wd_rows = jnp.broadcast_to(wd, (8, width))

    pre1 = (pre1_even, pre1_odd)
    pre2 = (pre2_even, pre2_odd)

    def first_layer(p, u):
        at_a = pl.ds(pl.multiple_of(p * span, span), LANES)
        at_b = pl.ds(pl.multiple_of(p * span + LANES, LANES), LANES)
        x = jnp.concatenate([x_ref[at_a, :], x_ref[at_b, :]], axis=1)
        pre1[u][...] = jnp.dot(x, w1f[...], preferred_element_type=F32)

    def first_act(p, u):
        h1, s1 = silu_pair(pre1[u][...])
        h1 = h1.astype(BF16)
        h1_ref[p] = h1
        h1t_ref[p] = h1.T
        s1_ref[p] = s1

    def second_layer(p, u):
        pre2[u][...] = jnp.dot(h1_ref[p], w2f[...], preferred_element_type=F32)

    def second_act(p, u):
        h2, s2 = silu_pair(pre2[u][...])
        h2 = h2.astype(BF16)
        h2_ref[p] = h2
        h2t_ref[p] = h2.T
        s2_ref[p] = s2

    def heads(p):
        left = []
        for k in range(2):
            hi, low = split_two(v_ref[pl.ds(pl.multiple_of((2 * p + k) * group, group), group), :])
            left += [side(hi, k), side(low, k), side(wd_rows, k)]
        left = jnp.concatenate(left, axis=0).astype(BF16)
        got = lax.dot_general(left, h2_ref[p], (((1,), (1,)), ((), ())), preferred_element_type=F32)
        for k in range(2):
            base = k * (2 * group + 8)
            dots = got[base : base + group] + got[base + group : base + 2 * group]
            q_ref[pl.ds(2 * p + k, 1), :] = jnp.sum(dots * group_mask, axis=0, keepdims=True)
            lg_ref[pl.ds(2 * p + k, 1), :] = got[base + 2 * group : base + 2 * group + 1]

    stages = (
        (4, lambda p, u: heads(p)),
        (3, second_act),
        (2, second_layer),
        (1, first_act),
        (0, first_layer),
    )

    def forward_step(p, u, static):
        for back, stage in stages:
            if not static or 0 <= p - back < pairs:
                stage(p - back, (u - back) % 2)

    def forward(i, carry):
        for u in range(2):
            forward_step(2 * i + u, u, False)
        return carry

    x_copy.wait()
    for p in range(4):
        forward_step(p, p % 2, True)
    lax.fori_loop(2, pairs // 2, forward, 0, unroll=True)
    for p in range(pairs, pairs + 4):
        forward_step(p, p % 2, True)

    spread = (iota((rays, LANES), 0) % group == iota((rays, LANES), 1) // per_ray).astype(BF16)
    gather = (iota((LANES, rays), 1) % group == iota((LANES, rays), 0) // per_ray).astype(BF16)
    owner = (iota((tiles, rays), 1) // group == iota((tiles, rays), 0)).astype(F32)
    from_s, to_s = iota((LANES, LANES), 0), iota((LANES, LANES), 1)
    same = from_s // per_ray == to_s // per_ray
    upto = (same & (from_s <= to_s)).astype(BF16)
    later = (same & (from_s > to_s)).astype(BF16)

    def to_samples(*ray_rows):
        out = dot_exact(jnp.concatenate([owner * r for r in ray_rows], axis=0), spread)
        return [out[i * tiles : (i + 1) * tiles] for i in range(len(ray_rows))]

    def to_rays(*sample_values):
        out = dot_exact(jnp.concatenate(sample_values, axis=0), gather)
        return [
            jnp.sum(out[i * tiles : (i + 1) * tiles] * owner, axis=0, keepdims=True)
            for i in range(len(sample_values))
        ]

    logits = lg_ref[...]
    q = q_ref[...]
    count, length = to_samples(count_ref[...].astype(F32), step_ref[...])
    is_valid = (iota((tiles, LANES), 1) % per_ray).astype(F32) < count
    softplus = jnp.maximum(logits, 0.0) + jnp.log1p(jnp.exp(-jnp.abs(logits)))
    depth_step = jnp.where(is_valid, softplus * length, 0.0)
    depth_incl = dot_exact(depth_step, upto)
    half_step = jnp.tanh(0.5 * depth_step)
    weights = jnp.exp(depth_step - depth_incl) * (2.0 * half_step / (1.0 + half_step))
    brick_depth, brick_dot = to_rays(depth_step, weights * q)
    ex_ref[0] = jnp.concatenate([brick_depth, brick_dot, jnp.zeros((6, rays), F32)], axis=0)

    pl.semaphore_wait(barrier, n_brick + n_ray - 2)

    def ex_copy(d):
        return pltpu.make_async_remote_copy(
            src_ref=ex_ref.at[0],
            dst_ref=ex_ref.at[d],
            send_sem=ex_send.at[d],
            recv_sem=ex_recv.at[d],
            device_id={"brick": lax.rem(my_brick + d, n_brick)},
            device_id_type=MESH,
        )

    for d in range(1, n_brick):
        ex_copy(d).start()

    def turn(p, carry):
        at_a = pl.ds(pl.multiple_of(p * span, span), LANES)
        at_b = pl.ds(pl.multiple_of(p * span + LANES, LANES), LANES)
        xt_ref[p] = jnp.concatenate([x_ref[at_a, :], x_ref[at_b, :]], axis=1).T
        return carry

    lax.fori_loop(0, pairs, turn, 0)
    w1b[...] = block_diag(w1_ref[0].astype(F32).T).astype(BF16)
    w2b[...] = block_diag(w2_ref[0].astype(F32).T * 0.5).astype(BF16)
    for d in range(1, n_brick):
        ex_copy(d).wait()

    def walk(order, is_past):
        gap = jnp.zeros((1, rays), F32)
        seen = jnp.zeros((1, rays), F32)
        for k in order:
            there = ex_ref[lax.rem(my_brick - k + n_brick, n_brick)]
            past = jnp.where(is_past(k), 1.0, 0.0)
            seen = seen + past * jnp.exp(-gap) * there[1:2]
            gap = gap + past * there[0:1]
        return gap, seen

    upper_depth, upper_seen = walk(range(n_brick), lambda k: k > my_brick)
    lower_depth, lower_seen = walk(range(n_brick - 1, -1, -1), lambda k: k < my_brick)
    flipped = flip_ref[...] > 0
    through_front = jnp.exp(-jnp.where(flipped, upper_depth, lower_depth))
    behind = jnp.where(flipped, lower_seen, upper_seen)
    front, brick_grad = to_samples(through_front, -through_front * jnp.exp(-brick_depth) * behind)
    own_grad = front * q
    later_sum = dot_exact(weights * own_grad, later)
    step_grad = jnp.exp(-depth_incl) * own_grad - later_sum + brick_grad
    sigmoid = 0.5 + 0.5 * jnp.tanh(0.5 * logits)
    lg_ref[...] = jnp.where(is_valid, step_grad * length * sigmoid, 0.0)
    c_ref[...] = front * weights

    unit = (iota((8, width), 1) == feat).astype(F32)

    def rows_of(pair):
        return jnp.concatenate([pair[:, :width], pair[:, width:]], axis=0)

    def contract_rows(left, right):
        return lax.dot_general(left, right, (((0,), (0,)), ((), ())), preferred_element_type=F32)

    def side_by_side(p):
        left, right = [], []
        for k in range(2):
            t = 2 * p + k
            c_hi, c_low = split_two(c_ref[pl.ds(t, 1), :] * group_mask)
            s_hi, s_low = split_two(sc_ref[pl.ds(pl.multiple_of(t * group, group), group), :])
            left += [c_hi, c_hi, c_low, lg_ref[pl.ds(t, 1), :] * group_mask]
            right += [side(s_hi, k), side(s_low, k), side(s_hi, k), side(unit, k)]
        return jnp.concatenate(left, axis=0).astype(BF16), jnp.concatenate(right, axis=0).astype(BF16)

    def halves_dot(left, right):
        return jnp.dot(left[:width], right[:, :width], preferred_element_type=F32) + jnp.dot(
            left[width:], right[:, width:], preferred_element_type=F32
        )

    def second_grads(p):
        acc[1] += halves_dot(h1t_ref[p], p2_ref[p])
        acc[2] += halves_dot(h2t_ref[p], fg_ref[p])

    def feature_grads(p):
        left, right = side_by_side(p)
        fg_ref[p] = contract_rows(left, right).astype(BF16)

    def back_two(p):
        h2g = jnp.dot(fg_ref[p], wfb[...], preferred_element_type=F32)
        p2_ref[p] = (h2g * s2_ref[p]).astype(BF16)

    def first_grads(p):
        acc[0] += halves_dot(xt_ref[p], p1_ref[p])

    def back_one(p):
        h1g = jnp.dot(p2_ref[p], w2b[...], preferred_element_type=F32)
        p1_ref[p] = (h1g * s1_ref[p]).astype(BF16)

    def pipelined(*stages):
        last = len(stages) - 1

        def step(p, static):
            for back in range(last, -1, -1):
                if not static or 0 <= p - back < pairs:
                    stages[back](p - back)

        def body(p, carry):
            step(p, False)
            return carry

        for p in range(last):
            step(p, True)
        lax.fori_loop(last, pairs, body, 0, unroll=UNROLL_BACK)
        for p in range(pairs, pairs + last):
            step(p, True)

    share = width // n_ray

    def red_copy(d, first):
        to = lax.rem(my_ray + d, n_ray)
        part = pl.ds(0, 1) if first else pl.ds(1, 2)
        sem = d + n_ray * first
        return pltpu.make_async_remote_copy(
            src_ref=acc.at[part, pl.ds(pl.multiple_of(to * share, share), share), :],
            dst_ref=red_ref.at[d, part],
            send_sem=red_send.at[sem],
            recv_sem=red_recv.at[sem],
            device_id={"ray": to},
            device_id_type=MESH,
        )

    pipelined(feature_grads, back_two, second_grads)
    for d in range(1, n_ray):
        red_copy(d, 0).start()
    pipelined(back_one, first_grads)
    for d in range(1, n_ray):
        red_copy(d, 1).start()

    def finish(p, carry):
        got = jnp.dot(p1_ref[p], w1b[...], preferred_element_type=F32).astype(BF16)
        o_ref[pl.ds(pl.multiple_of(p * span, span), span), :] = rows_of(got)
        out_copy(p).start()
        return carry

    lax.fori_loop(0, pairs, finish, 0, unroll=True)

    total = acc[:, pl.ds(pl.multiple_of(my_ray * share, share), share), :]
    for d in range(1, n_ray):
        red_copy(d, 0).wait()
        red_copy(d, 1).wait()
        total = total + red_ref[d]
    total = total * (1.0 / LOSS_SCALE)
    g1_ref[0] = total[0]
    g2_ref[0] = total[1]
    g3_ref[0] = total[2][:, :feat]
    g4_ref[...] = total[2].T[feat : feat + 1, :]

    @pl.loop(0, pairs)
    def _(p):
        out_copy(p).wait()


def hand_out(big_in, *refs):
    small_in, big_out, small_out, held, in_sem, out_sem, sems = (
        refs[:4],
        refs[4],
        refs[5:9],
        refs[9],
        refs[10],
        refs[11],
        refs[12],
    )
    size = held.shape[0] // PIECES
    pieces = [pl.ds(i * size, size) for i in range(PIECES)]
    arrive = [pltpu.make_async_copy(big_in.at[at], held.at[at], in_sem.at[i]) for i, at in enumerate(pieces)]
    leave = [pltpu.make_async_copy(held.at[at], big_out.at[at], out_sem.at[i]) for i, at in enumerate(pieces)]
    small = [pltpu.make_async_copy(small_in[i], small_out[i], sems.at[i]) for i in range(4)]
    for copy in arrive:
        copy.start()
    for copy in small:
        copy.start()
    for i in range(PIECES):
        arrive[i].wait()
        leave[i].start()
    for copy in leave + small:
        copy.wait()


def solution(mesh):
    n_brick, n_ray = mesh.shape["brick"], mesh.shape["ray"]

    def shards(samples_in, sample_count, step_length, view_flip, pixel_grad, w1, w2, wf, wd):
        rays, _, per_ray, width = samples_in.shape
        feat = pixel_grad.shape[0]
        rows = rays * per_ray
        pairs = rows // (2 * LANES)
        tiles = rows // LANES
        share = width // n_ray
        vmem = pl.BlockSpec(memory_space=pltpu.VMEM)
        hbm = pl.BlockSpec(memory_space=pl.ANY)
        pair_shape = (pairs, LANES, 2 * width)
        outs = pl.pallas_call(
            functools.partial(kernel, n_brick, n_ray, per_ray),
            out_shape=(
                jax.ShapeDtypeStruct((rows, width), BF16),
                jax.ShapeDtypeStruct((1, share, width), F32),
                jax.ShapeDtypeStruct((1, share, width), F32),
                jax.ShapeDtypeStruct((1, share, feat), F32),
                jax.ShapeDtypeStruct((1, share), F32),
            ),
            in_specs=[hbm] + [vmem] * 8,
            out_specs=(hbm,) + (vmem,) * 4,
            scratch_shapes=[
                pltpu.VMEM((rows, width), BF16),
                pltpu.VMEM((rows, width), BF16),
                pltpu.VMEM(pair_shape, BF16),
                pltpu.VMEM(pair_shape, BF16),
                pltpu.VMEM((pairs, 2 * width, LANES), BF16),
                pltpu.VMEM((pairs, 2 * width, LANES), BF16),
                pltpu.VMEM((pairs, 2 * width, LANES), BF16),
                pltpu.VMEM(pair_shape[1:], F32),
                pltpu.VMEM(pair_shape[1:], F32),
                pltpu.VMEM(pair_shape[1:], F32),
                pltpu.VMEM(pair_shape[1:], F32),
                pltpu.VMEM(pair_shape, F32),
                pltpu.VMEM(pair_shape, F32),
                pltpu.VMEM(pair_shape, BF16),
                pltpu.VMEM(pair_shape, BF16),
                pltpu.VMEM(pair_shape, BF16),
                pltpu.VMEM((rays, width), F32),
                pltpu.VMEM((rays, width), F32),
                pltpu.VMEM((tiles, LANES), F32),
                pltpu.VMEM((tiles, LANES), F32),
                pltpu.VMEM((tiles, LANES), F32),
                pltpu.VMEM((2 * width, 2 * width), BF16),
                pltpu.VMEM((2 * width, 2 * width), BF16),
                pltpu.VMEM((2 * width, 2 * width), BF16),
                pltpu.VMEM((2 * width, 2 * width), BF16),
                pltpu.VMEM((2 * width, 2 * width), BF16),
                pltpu.VMEM((3, width, width), F32),
                pltpu.VMEM((n_brick, 8, rays), F32),
                pltpu.VMEM((n_ray, 3, share, width), F32),
                pltpu.SemaphoreType.DMA,
                pltpu.SemaphoreType.DMA((pairs,)),
                pltpu.SemaphoreType.DMA((n_brick,)),
                pltpu.SemaphoreType.DMA((n_brick,)),
                pltpu.SemaphoreType.DMA((2 * n_ray,)),
                pltpu.SemaphoreType.DMA((2 * n_ray,)),
            ],
            compiler_params=pltpu.CompilerParams(
                collective_id=0, has_side_effects=True
            ),
        )(
            samples_in.reshape(rows, width),
            sample_count.reshape(1, rays),
            step_length.reshape(1, rays),
            view_flip.reshape(1, rays),
            pixel_grad,
            w1,
            w2,
            jnp.swapaxes(wf, 1, 2),
            wd,
        )
        outs = pl.pallas_call(
            hand_out,
            out_shape=tuple(jax.ShapeDtypeStruct(o.shape, o.dtype) for o in outs),
            in_specs=[hbm] + [vmem] * 4,
            out_specs=(hbm,) * 5,
            scratch_shapes=[
                pltpu.VMEM((rows, width), BF16),
                pltpu.SemaphoreType.DMA((PIECES,)),
                pltpu.SemaphoreType.DMA((PIECES,)),
                pltpu.SemaphoreType.DMA((4,)),
            ],
        )(*outs)
        return (outs[0].reshape(samples_in.shape),) + tuple(outs[1:])

    placed = (
        P(("groups", "ray"), "brick", None, None),
        P(("groups", "ray"), "brick"),
        P(("groups", "ray")),
        P(("groups", "ray")),
        P(None, ("groups", "ray")),
        P("brick", None, None),
        P("brick", None, None),
        P("brick", None, None),
        P("brick", None),
    )
    return jax.shard_map(
        shards,
        mesh=mesh,
        in_specs=placed,
        out_specs=(
            P(("groups", "ray"), "brick", None, None),
            P(("groups", "brick"), "ray", None),
            P(("groups", "brick"), "ray", None),
            P(("groups", "brick"), "ray", None),
            P(("groups", "brick"), "ray"),
        ),
        check_vma=False,
    )
```

```python
import functools

import jax
import jax.numpy as jnp
from jax import lax
from jax.experimental import pallas as pl
from jax.experimental.pallas import tpu as pltpu
from jax.sharding import PartitionSpec as P

LOSS_SCALE = 1024.0
LANES = 256
CHUNKS = 1
X_PIECES = 4
K_TILES = 8
F32 = jnp.float32
BF16 = jnp.bfloat16
MESH = pl.DeviceIdType.MESH


def iota(shape, dim):
    return lax.broadcasted_iota(jnp.int32, shape, dim)


def split_two(v):
    hi = v.astype(BF16).astype(F32)
    return hi, v - hi


def split_three(v):
    hi, rest = split_two(v)
    mid, low = split_two(rest)
    return hi, mid, low


def dot_exact(v, m):
    rows = v.shape[0]
    out = jnp.dot(
        jnp.concatenate(split_three(v), axis=0).astype(BF16), m, preferred_element_type=F32
    )
    return out[:rows] + out[rows : 2 * rows] + out[2 * rows :]


def contract_rows(left, right):
    return lax.dot_general(left, right, (((0,), (0,)), ((), ())), preferred_element_type=F32)


def block_diag(w):
    z = jnp.zeros_like(w)
    return jnp.concatenate(
        [jnp.concatenate([w, z], axis=1), jnp.concatenate([z, w], axis=1)], axis=0
    )


def side(v, right):
    z = jnp.zeros_like(v)
    return jnp.concatenate([z, v] if right else [v, z], axis=1)


def silu_pair(half):
    t = jnp.tanh(half)
    a = 1.0 + t
    h = half * a
    slope = a + h * (1.0 - t)
    return h, slope


def kernel(
    n_brick,
    n_ray,
    per_ray,
    x_hbm,
    count_hbm,
    step_hbm,
    flip_hbm,
    pg_hbm,
    w1_hbm,
    w2_hbm,
    wf_hbm,
    wd_hbm,
    o_ref,
    g1_ref,
    g2_ref,
    g3_ref,
    g4_ref,
    x_ref,
    count_ref,
    step_ref,
    flip_ref,
    pg_ref,
    w1_ref,
    w2_ref,
    wf_ref,
    wd_ref,
    xt_ref,
    h1_ref,
    h1t_ref,
    h2_ref,
    p1_ref,
    p2_ref,
    s1_ref,
    s2_ref,
    v_ref,
    sc_ref,
    q_ref,
    lg_ref,
    len_ref,
    c_ref,
    u_ref,
    w1f,
    w2f,
    w1b,
    w2b,
    wfb,
    acc,
    ex_ref,
    red_ref,
    in_sem,
    x_sem,
    ex_send,
    ex_recv,
    red_send,
    red_recv,
):
    rows, width = x_ref.shape
    feat, rays = pg_ref.shape
    group = LANES // per_ray
    tiles = rows // LANES
    pairs = tiles // 2
    span = 2 * LANES
    half = LANES // 2

    small = [
        pltpu.make_async_copy(src, dst, in_sem.at[i])
        for i, (src, dst) in enumerate(
            (
                (w1_hbm, w1_ref),
                (w2_hbm, w2_ref),
                (wf_hbm, wf_ref),
                (wd_hbm, wd_ref),
                (pg_hbm, pg_ref),
                (count_hbm, count_ref),
                (step_hbm, step_ref),
                (flip_hbm, flip_ref),
            )
        )
    ]
    piece = rows // X_PIECES
    pieces = [
        pltpu.make_async_copy(
            x_hbm.at[pl.ds(i * piece, piece)], x_ref.at[pl.ds(i * piece, piece)], x_sem.at[i]
        )
        for i in range(X_PIECES)
    ]
    small[0].start()
    pieces[0].start()
    for copy in small[1:] + pieces[1:]:
        copy.start()

    my_brick = lax.axis_index("brick")
    my_ray = lax.axis_index("ray")
    barrier = pltpu.get_barrier_semaphore()
    for d in range(1, n_brick):
        pl.semaphore_signal(
            barrier, inc=1, device_id={"brick": lax.rem(my_brick + d, n_brick)}, device_id_type=MESH
        )
    for d in range(1, n_ray):
        pl.semaphore_signal(
            barrier, inc=1, device_id={"ray": lax.rem(my_ray + d, n_ray)}, device_id_type=MESH
        )

    group_mask = (iota((group, LANES), 0) == iota((group, LANES), 1) // per_ray).astype(F32)
    unit = (iota((8, width), 1) == feat).astype(F32)
    rays_c = rays // CHUNKS
    tiles_c = tiles // CHUNKS
    pairs_c = pairs // CHUNKS
    spread = (iota((rays_c, LANES), 0) % group == iota((rays_c, LANES), 1) // per_ray).astype(BF16)
    gather = (iota((LANES, rays_c), 1) % group == iota((LANES, rays_c), 0) // per_ray).astype(BF16)
    owner = (iota((tiles_c, rays_c), 1) // group == iota((tiles_c, rays_c), 0)).astype(F32)
    from_s, to_s = iota((LANES, LANES), 0), iota((LANES, LANES), 1)
    same = from_s // per_ray == to_s // per_ray
    upto = (same & (from_s <= to_s)).astype(BF16)
    later = (same & (from_s > to_s)).astype(BF16)

    def to_samples(*ray_rows):
        out = dot_exact(jnp.concatenate([owner * r for r in ray_rows], axis=0), spread)
        return [out[i * tiles_c : (i + 1) * tiles_c] for i in range(len(ray_rows))]

    def to_rays(*sample_values):
        out = dot_exact(jnp.concatenate(sample_values, axis=0), gather)
        return [
            jnp.sum(out[i * tiles_c : (i + 1) * tiles_c] * owner, axis=0, keepdims=True)
            for i in range(len(sample_values))
        ]

    small[0].wait()
    w1 = w1_ref[0].astype(F32)
    w1f[...] = block_diag(w1 * 0.5).astype(BF16)

    def pair_of(ref, p):
        return jnp.concatenate([ref[2 * p], ref[2 * p + 1]], axis=1)

    def put_pair(ref, p, v):
        ref[2 * p] = v[:, :width]
        ref[2 * p + 1] = v[:, width:]

    def put_turned(ref, p, v):
        for k in range(2):
            t = v[:, k * width : (k + 1) * width].T
            for j in range(2):
                ref[2 * p + k, j] = t[:, j * half : (j + 1) * half]

    def first_layer(p):
        if p % (pairs // X_PIECES) == 0:
            pieces[p // (pairs // X_PIECES)].wait()
        x = jnp.concatenate(
            [x_ref[pl.ds(p * span, LANES), :], x_ref[pl.ds(p * span + LANES, LANES), :]], axis=1
        )
        h1, s1 = silu_pair(jnp.dot(x, w1f[...], preferred_element_type=F32))
        h1 = h1.astype(BF16)
        put_pair(h1_ref, p, h1)
        s1_ref[p] = s1
        put_turned(h1t_ref, p, h1)
        put_turned(xt_ref, p, x)

    def second_layer(p):
        h2, s2 = silu_pair(jnp.dot(pair_of(h1_ref, p), w2f[...], preferred_element_type=F32))
        put_pair(h2_ref, p, h2.astype(BF16))
        s2_ref[p] = s2

    def heads(p):
        left = []
        for k in range(2):
            hi, low = split_two(v_ref[pl.ds((2 * p + k) * group, group), :])
            left += [side(hi, k), side(low, k), side(wd_rows, k)]
        left = jnp.concatenate(left, axis=0).astype(BF16)
        got = lax.dot_general(
            left, pair_of(h2_ref, p), (((1,), (1,)), ((), ())), preferred_element_type=F32
        )
        for k in range(2):
            base = k * (2 * group + 8)
            dots = got[base : base + group] + got[base + group : base + 2 * group]
            q_ref[pl.ds(2 * p + k, 1), :] = jnp.sum(dots * group_mask, axis=0, keepdims=True)
            lg_ref[pl.ds(2 * p + k, 1), :] = got[base + 2 * group : base + 2 * group + 1]

    first_layer(0)
    for copy in small[1:]:
        copy.wait()
    w2 = w2_ref[0].astype(F32)
    wd = wd_ref[...].astype(F32)
    w2f[...] = block_diag(w2 * 0.5).astype(BF16)
    wide = jnp.concatenate(
        [wf_ref[0].astype(F32), wd, jnp.zeros((width - feat - 1, width), F32)], axis=0
    )
    wfb[...] = block_diag(wide * 0.5).astype(BF16)
    w1b[...] = block_diag(w1.T).astype(BF16)
    w2b[...] = block_diag(w2.T * 0.5).astype(BF16)
    scaled = jnp.concatenate(
        [LOSS_SCALE * pg_ref[...], jnp.zeros((width - feat, rays), F32)], axis=0
    ).T
    sc_ref[...] = scaled
    v_ref[...] = dot_exact(scaled, wide.astype(BF16))
    wd_rows = jnp.broadcast_to(wd, (8, width))
    for ch in range(CHUNKS):
        at = slice(ch * rays_c, (ch + 1) * rays_c)
        count, length = to_samples(count_ref[:, at].astype(F32), step_ref[:, at])
        len_ref[pl.ds(ch * tiles_c, tiles_c), :] = jnp.where(
            (iota((tiles_c, LANES), 1) % per_ray).astype(F32) < count, length, 0.0
        )

    def middle(ch):
        mine = pl.ds(ch * tiles_c, tiles_c)
        logits = lg_ref[mine, :]
        q = q_ref[mine, :]
        length = len_ref[mine, :]
        softplus = jnp.maximum(logits, 0.0) + jnp.log1p(jnp.exp(-jnp.abs(logits)))
        depth_step = softplus * length
        depth_incl = dot_exact(depth_step, upto)
        half_step = jnp.tanh(0.5 * depth_step)
        weights = jnp.exp(depth_step - depth_incl) * (2.0 * half_step / (1.0 + half_step))
        weighted = weights * q
        brick_depth, brick_dot = to_rays(depth_step, weighted)
        ex_ref[ch, 0] = jnp.concatenate([brick_depth, brick_dot, jnp.zeros((6, rays_c), F32)], axis=0)
        c_ref[mine, :] = weights
        q_ref[mine, :] = jnp.exp(-depth_incl) * q - dot_exact(weighted, later)
        len_ref[mine, :] = length * (0.5 + 0.5 * jnp.tanh(0.5 * logits))

    def ex_copy(ch, d):
        return pltpu.make_async_remote_copy(
            src_ref=ex_ref.at[ch, 0],
            dst_ref=ex_ref.at[ch, d],
            send_sem=ex_send.at[ch, d],
            recv_sem=ex_recv.at[ch, d],
            device_id={"brick": lax.rem(my_brick + d, n_brick)},
            device_id_type=MESH,
        )

    def send(ch):
        if ch == 0:
            pl.semaphore_wait(barrier, n_brick + n_ray - 2)
        for d in range(1, n_brick):
            ex_copy(ch, d).start()

    def composite(ch):
        for d in range(1, n_brick):
            ex_copy(ch, d).wait()
        mine = pl.ds(ch * tiles_c, tiles_c)
        there = [ex_ref[ch, lax.rem(my_brick - k + n_brick, n_brick)] for k in range(n_brick)]

        def walk(order, is_past):
            gap = jnp.zeros((1, rays_c), F32)
            seen = jnp.zeros((1, rays_c), F32)
            for k in order:
                past = jnp.where(is_past(k), 1.0, 0.0)
                seen = seen + past * jnp.exp(-gap) * there[k][1:2]
                gap = gap + past * there[k][0:1]
            return gap, seen

        upper_depth, upper_seen = walk(range(n_brick), lambda k: k > my_brick)
        lower_depth, lower_seen = walk(range(n_brick - 1, -1, -1), lambda k: k < my_brick)
        flipped = flip_ref[:, ch * rays_c : (ch + 1) * rays_c] > 0
        through_front = jnp.exp(-jnp.where(flipped, upper_depth, lower_depth))
        behind = jnp.where(flipped, lower_seen, upper_seen)
        brick_depth = ex_ref[ch, 0, 0:1]
        front, brick_grad = to_samples(
            through_front, -through_front * jnp.exp(-brick_depth) * behind
        )
        lg_ref[mine, :] = (front * q_ref[mine, :] + brick_grad) * len_ref[mine, :]
        c_ref[mine, :] = front * c_ref[mine, :]

    def feature_grads(p):
        left, right = [], []
        sums = []
        for k in range(2):
            t = 2 * p + k
            c_hi, c_low = split_two(c_ref[pl.ds(t, 1), :] * group_mask)
            lgm = lg_ref[pl.ds(t, 1), :] * group_mask
            s_hi, s_low = split_two(sc_ref[pl.ds(t * group, group), :])
            left += [c_hi, c_hi, c_low, lgm]
            sums += [c_hi, c_low, lgm]
            right += [side(s_hi, k), side(s_low, k), side(s_hi, k), side(unit, k)]
        left = jnp.concatenate(left, axis=0).astype(BF16)
        right = jnp.concatenate(right, axis=0).astype(BF16)
        sums = jnp.concatenate(sums, axis=0).astype(BF16)
        fg = contract_rows(left, right).astype(BF16)
        h2g = jnp.dot(fg, wfb[...], preferred_element_type=F32)
        put_pair(p2_ref, p, (h2g * s2_ref[p]).astype(BF16))
        got = jnp.dot(sums, pair_of(h2_ref, p), preferred_element_type=F32)
        dens = jnp.zeros((group, width), F32)
        for k in range(2):
            base = 3 * group * k
            mine = got[:, k * width : (k + 1) * width]
            u_ref[pl.ds((2 * p + k) * group, group), :] = (
                mine[base : base + group] + mine[base + group : base + 2 * group]
            )
            dens = dens + mine[base + 2 * group : base + 3 * group]
        return dens

    def back_one(p):
        h1g = jnp.dot(pair_of(p2_ref, p), w2b[...], preferred_element_type=F32)
        put_pair(p1_ref, p, (h1g * s1_ref[p]).astype(BF16))

    def finish(p):
        got = jnp.dot(pair_of(p1_ref, p), w1b[...], preferred_element_type=F32).astype(BF16)
        o_ref[pl.ds(p * span, LANES), :] = got[:, :width]
        o_ref[pl.ds(p * span + LANES, LANES), :] = got[:, width:]

    def weight_grad(turned, grads):
        total = None
        for t0 in range(0, tiles, K_TILES):
            left = jnp.concatenate(
                [turned[t, j] for t in range(t0, t0 + K_TILES) for j in range(2)], axis=1
            )
            right = grads[pl.ds(t0, K_TILES)].reshape(K_TILES * LANES, width)
            got = jnp.dot(left, right, preferred_element_type=F32)
            total = got if total is None else total + got
        return total

    share = width // n_ray

    def red_copy(d, first):
        to = lax.rem(my_ray + d, n_ray)
        part = pl.ds(0, 1) if first else pl.ds(1, 2)
        sem = d + n_ray * first
        return pltpu.make_async_remote_copy(
            src_ref=acc.at[part, pl.ds(pl.multiple_of(to * share, share), share), :],
            dst_ref=red_ref.at[d, part],
            send_sem=red_send.at[sem],
            recv_sem=red_recv.at[sem],
            device_id={"ray": to},
            device_id_type=MESH,
        )

    for p in range(1, pairs + 2):
        if p < pairs:
            first_layer(p)
        if p - 1 < pairs:
            second_layer(p - 1)
        if p - 2 >= 0:
            heads(p - 2)
        for ch in range(CHUNKS):
            if p - 2 == (ch + 1) * pairs_c - 1:
                middle(ch)
                send(ch)

    dens = jnp.zeros((group, width), F32)
    for p in range(pairs + 1):
        if p % pairs_c == 0 and p < pairs:
            composite(p // pairs_c)
        if p < pairs:
            dens = dens + feature_grads(p)
        if p >= 1:
            back_one(p - 1)
    acc[1] = weight_grad(h1t_ref, p2_ref)
    u_hi, u_low = split_two(u_ref[...])
    s_hi, s_low = split_two(sc_ref[...])
    parts = split_three(dens)
    acc[2] = contract_rows(
        jnp.concatenate([u_hi, u_hi, u_low, *parts], axis=0).astype(BF16),
        jnp.concatenate([s_hi, s_low, s_hi, unit, unit, unit], axis=0).astype(BF16),
    )
    for d in range(1, n_ray):
        red_copy(d, 0).start()
    acc[0] = weight_grad(xt_ref, p1_ref)
    for d in range(1, n_ray):
        red_copy(d, 1).start()
    for p in range(pairs):
        finish(p)

    total = acc[:, pl.ds(pl.multiple_of(my_ray * share, share), share), :]
    for d in range(1, n_ray):
        red_copy(d, 0).wait()
        red_copy(d, 1).wait()
        total = total + red_ref[d]
    total = total * (1.0 / LOSS_SCALE)
    g1_ref[0] = total[0]
    g2_ref[0] = total[1]
    g3_ref[0] = total[2][:, :feat]
    g4_ref[...] = total[2].T[feat : feat + 1, :]


def hand_out(*refs):
    held, out, sems = refs[:5], refs[5:10], refs[10]
    copies = [pltpu.make_async_copy(held[i], out[i], sems.at[i]) for i in range(5)]
    for copy in copies:
        copy.start()
    for copy in copies:
        copy.wait()


def solution(mesh):
    n_brick, n_ray = mesh.shape["brick"], mesh.shape["ray"]

    def shards(samples_in, sample_count, step_length, view_flip, pixel_grad, w1, w2, wf, wd):
        rays, _, per_ray, width = samples_in.shape
        feat = pixel_grad.shape[0]
        rows = rays * per_ray
        pairs = rows // (2 * LANES)
        tiles = rows // LANES
        share = width // n_ray
        vmem = pl.BlockSpec(memory_space=pltpu.VMEM)
        hbm = pl.BlockSpec(memory_space=pl.ANY)
        tile_shape = (tiles, LANES, width)
        turned_shape = (tiles, 2, width, LANES // 2)
        outs = pl.pallas_call(
            functools.partial(kernel, n_brick, n_ray, per_ray),
            out_shape=(
                pltpu.VMEM((rows, width), BF16),
                pltpu.VMEM((1, share, width), F32),
                pltpu.VMEM((1, share, width), F32),
                pltpu.VMEM((1, share, feat), F32),
                pltpu.VMEM((1, share), F32),
            ),
            in_specs=[hbm] * 9,
            out_specs=(vmem,) * 5,
            scratch_shapes=[
                pltpu.VMEM((rows, width), BF16),
                pltpu.VMEM((1, rays), jnp.int32),
                pltpu.VMEM((1, rays), F32),
                pltpu.VMEM((1, rays), jnp.int32),
                pltpu.VMEM((feat, rays), F32),
                pltpu.VMEM((1, width, width), BF16),
                pltpu.VMEM((1, width, width), BF16),
                pltpu.VMEM((1, feat, width), BF16),
                pltpu.VMEM((1, width), BF16),
                pltpu.VMEM(turned_shape, BF16),
                pltpu.VMEM(tile_shape, BF16),
                pltpu.VMEM(turned_shape, BF16),
                pltpu.VMEM(tile_shape, BF16),
                pltpu.VMEM(tile_shape, BF16),
                pltpu.VMEM(tile_shape, BF16),
                pltpu.VMEM((pairs, LANES, 2 * width), F32),
                pltpu.VMEM((pairs, LANES, 2 * width), F32),
                pltpu.VMEM((rays, width), F32),
                pltpu.VMEM((rays, width), F32),
                pltpu.VMEM((tiles, LANES), F32),
                pltpu.VMEM((tiles, LANES), F32),
                pltpu.VMEM((tiles, LANES), F32),
                pltpu.VMEM((tiles, LANES), F32),
                pltpu.VMEM((rays, width), F32),
                pltpu.VMEM((2 * width, 2 * width), BF16),
                pltpu.VMEM((2 * width, 2 * width), BF16),
                pltpu.VMEM((2 * width, 2 * width), BF16),
                pltpu.VMEM((2 * width, 2 * width), BF16),
                pltpu.VMEM((2 * width, 2 * width), BF16),
                pltpu.VMEM((3, width, width), F32),
                pltpu.VMEM((CHUNKS, n_brick, 8, rays // CHUNKS), F32),
                pltpu.VMEM((n_ray, 3, share, width), F32),
                pltpu.SemaphoreType.DMA((8,)),
                pltpu.SemaphoreType.DMA((X_PIECES,)),
                pltpu.SemaphoreType.DMA((CHUNKS, n_brick)),
                pltpu.SemaphoreType.DMA((CHUNKS, n_brick)),
                pltpu.SemaphoreType.DMA((2 * n_ray,)),
                pltpu.SemaphoreType.DMA((2 * n_ray,)),
            ],
            compiler_params=pltpu.CompilerParams(
                collective_id=0, has_side_effects=True, vmem_limit_bytes=52 * 1024 * 1024
            ),
        )(
            samples_in.reshape(rows, width),
            sample_count.reshape(1, rays),
            step_length.reshape(1, rays),
            view_flip.reshape(1, rays),
            pixel_grad,
            w1,
            w2,
            jnp.swapaxes(wf, 1, 2),
            wd,
        )
        outs = pl.pallas_call(
            hand_out,
            out_shape=tuple(jax.ShapeDtypeStruct(o.shape, o.dtype) for o in outs),
            in_specs=[vmem] * 5,
            out_specs=(hbm,) * 5,
            scratch_shapes=[pltpu.SemaphoreType.DMA((5,))],
            compiler_params=pltpu.CompilerParams(vmem_limit_bytes=4 * 1024 * 1024),
        )(*[pltpu.with_memory_space_constraint(o, pltpu.VMEM) for o in outs])
        return (outs[0].reshape(samples_in.shape),) + tuple(outs[1:])

    placed = (
        P(("groups", "ray"), "brick", None, None),
        P(("groups", "ray"), "brick"),
        P(("groups", "ray")),
        P(("groups", "ray")),
        P(None, ("groups", "ray")),
        P("brick", None, None),
        P("brick", None, None),
        P("brick", None, None),
        P("brick", None),
    )
    return jax.shard_map(
        shards,
        mesh=mesh,
        in_specs=placed,
        out_specs=(
            P(("groups", "ray"), "brick", None, None),
            P(("groups", "brick"), "ray", None),
            P(("groups", "brick"), "ray", None),
            P(("groups", "brick"), "ray", None),
            P(("groups", "brick"), "ray"),
        ),
        check_vma=False,
    )
```

```python
import functools

import jax
import jax.numpy as jnp
from jax import lax
from jax.experimental import pallas as pl
from jax.experimental.pallas import tpu as pltpu
from jax.sharding import PartitionSpec as P

LOSS_SCALE = 1024.0
LANES = 256
CHUNKS = 2
K_TILES = 8
HEAD_START = 3
F32 = jnp.float32
BF16 = jnp.bfloat16
MESH = pl.DeviceIdType.MESH


def iota(shape, dim):
    return lax.broadcasted_iota(jnp.int32, shape, dim)


def split_two(v):
    hi = v.astype(BF16).astype(F32)
    return hi, v - hi


def split_three(v):
    hi, rest = split_two(v)
    mid, low = split_two(rest)
    return hi, mid, low


def dot_exact(v, m):
    rows = v.shape[0]
    out = jnp.dot(
        jnp.concatenate(split_three(v), axis=0).astype(BF16), m, preferred_element_type=F32
    )
    return out[:rows] + out[rows : 2 * rows] + out[2 * rows :]


def contract_rows(left, right):
    return lax.dot_general(left, right, (((0,), (0,)), ((), ())), preferred_element_type=F32)


def block_diag(w):
    z = jnp.zeros_like(w)
    return jnp.concatenate(
        [jnp.concatenate([w, z], axis=1), jnp.concatenate([z, w], axis=1)], axis=0
    )


def side(v, right):
    z = jnp.zeros_like(v)
    return jnp.concatenate([z, v] if right else [v, z], axis=1)


def silu_pair(half):
    t = jnp.tanh(half)
    a = 1.0 + t
    h = half * a
    slope = a + h * (1.0 - t)
    return h, slope


def kernel(
    n_brick,
    n_ray,
    per_ray,
    x_hbm,
    count_hbm,
    step_hbm,
    flip_hbm,
    pg_hbm,
    w1_hbm,
    w2_hbm,
    wf_hbm,
    wd_hbm,
    o_ref,
    g1_ref,
    g2_ref,
    g3_ref,
    g4_ref,
    x_ref,
    count_ref,
    step_ref,
    flip_ref,
    pg_ref,
    w1_ref,
    w2_ref,
    wf_ref,
    wd_ref,
    xt_ref,
    h1_ref,
    h1t_ref,
    h2_ref,
    p1_ref,
    p2_ref,
    s1_ref,
    s2_ref,
    v_ref,
    sc_ref,
    q_ref,
    lg_ref,
    len_ref,
    c_ref,
    u_ref,
    w1f,
    w2f,
    w1b,
    w2b,
    wfb,
    acc,
    ex_ref,
    red_ref,
    in_sem,
    x_sem,
    ex_send,
    ex_recv,
    red_send,
    red_recv,
):
    rows, width = x_ref.shape
    feat, rays = pg_ref.shape
    group = LANES // per_ray
    tiles = rows // LANES
    pairs = tiles // 2
    span = 2 * LANES
    half = LANES // 2

    small = [
        pltpu.make_async_copy(src, dst, in_sem.at[i])
        for i, (src, dst) in enumerate(
            (
                (w1_hbm, w1_ref),
                (w2_hbm, w2_ref),
                (wf_hbm, wf_ref),
                (wd_hbm, wd_ref),
                (pg_hbm, pg_ref),
                (count_hbm, count_ref),
                (step_hbm, step_ref),
                (flip_hbm, flip_ref),
            )
        )
    ]
    piece = rows // CHUNKS
    pieces = [
        pltpu.make_async_copy(
            x_hbm.at[pl.ds(i * piece, piece)], x_ref.at[pl.ds(i * piece, piece)], x_sem.at[i]
        )
        for i in range(CHUNKS)
    ]
    small[0].start()
    pieces[0].start()
    for copy in small[1:] + pieces[1:]:
        copy.start()

    my_brick = lax.axis_index("brick")
    my_ray = lax.axis_index("ray")
    barrier = pltpu.get_barrier_semaphore()
    for d in range(1, n_brick):
        pl.semaphore_signal(
            barrier, inc=1, device_id={"brick": lax.rem(my_brick + d, n_brick)}, device_id_type=MESH
        )
    for d in range(1, n_ray):
        pl.semaphore_signal(
            barrier, inc=1, device_id={"ray": lax.rem(my_ray + d, n_ray)}, device_id_type=MESH
        )

    group_mask = (iota((group, LANES), 0) == iota((group, LANES), 1) // per_ray).astype(F32)
    unit = (iota((8, width), 1) == feat).astype(F32)
    rays_c = rays // CHUNKS
    tiles_c = tiles // CHUNKS
    pairs_c = pairs // CHUNKS
    spread = (iota((rays_c, LANES), 0) % group == iota((rays_c, LANES), 1) // per_ray).astype(BF16)
    gather = (iota((LANES, rays_c), 1) % group == iota((LANES, rays_c), 0) // per_ray).astype(BF16)
    owner = (iota((tiles_c, rays_c), 1) // group == iota((tiles_c, rays_c), 0)).astype(F32)
    from_s, to_s = iota((LANES, LANES), 0), iota((LANES, LANES), 1)
    same = from_s // per_ray == to_s // per_ray
    upto = (same & (from_s <= to_s)).astype(BF16)
    later = (same & (from_s > to_s)).astype(BF16)

    def to_samples(*ray_rows):
        out = dot_exact(jnp.concatenate([owner * r for r in ray_rows], axis=0), spread)
        return [out[i * tiles_c : (i + 1) * tiles_c] for i in range(len(ray_rows))]

    def to_rays(*sample_values):
        out = dot_exact(jnp.concatenate(sample_values, axis=0), gather)
        return [
            jnp.sum(out[i * tiles_c : (i + 1) * tiles_c] * owner, axis=0, keepdims=True)
            for i in range(len(sample_values))
        ]

    for copy in small:
        copy.wait()
    w1 = w1_ref[0].astype(F32)
    w1f[...] = block_diag(w1 * 0.5).astype(BF16)

    def pair_of(ref, p):
        return jnp.concatenate([ref[2 * p], ref[2 * p + 1]], axis=1)

    def put_pair(ref, p, v):
        ref[2 * p] = v[:, :width]
        ref[2 * p + 1] = v[:, width:]

    def put_turned(ref, p, v):
        for k in range(2):
            ref[2 * p + k] = v[:, k * width : (k + 1) * width].T

    def x_pair(p):
        return jnp.concatenate(
            [x_ref[pl.ds(p * span, LANES), :], x_ref[pl.ds(p * span + LANES, LANES), :]], axis=1
        )

    def first_layer(p):
        h1, s1 = silu_pair(jnp.dot(x_pair(p), w1f[...], preferred_element_type=F32))
        put_pair(h1_ref, p, h1.astype(BF16))
        s1_ref[p] = s1

    def turn(p):
        put_turned(h1t_ref, p, pair_of(h1_ref, p))
        put_turned(xt_ref, p, x_pair(p))

    def second_layer(p):
        h2, s2 = silu_pair(jnp.dot(pair_of(h1_ref, p), w2f[...], preferred_element_type=F32))
        put_pair(h2_ref, p, h2.astype(BF16))
        s2_ref[p] = s2

    def heads(p):
        left = []
        for k in range(2):
            hi, low = split_two(v_ref[pl.ds((2 * p + k) * group, group), :])
            left += [side(hi, k), side(low, k), side(wd_rows, k)]
        left = jnp.concatenate(left, axis=0).astype(BF16)
        got = lax.dot_general(
            left, pair_of(h2_ref, p), (((1,), (1,)), ((), ())), preferred_element_type=F32
        )
        for k in range(2):
            base = k * (2 * group + 8)
            dots = got[base : base + group] + got[base + group : base + 2 * group]
            q_ref[pl.ds(2 * p + k, 1), :] = jnp.sum(dots * group_mask, axis=0, keepdims=True)
            lg_ref[pl.ds(2 * p + k, 1), :] = got[base + 2 * group : base + 2 * group + 1]

    w2 = w2_ref[0].astype(F32)
    wd = wd_ref[...].astype(F32)
    w2f[...] = block_diag(w2 * 0.5).astype(BF16)
    wide = jnp.concatenate(
        [wf_ref[0].astype(F32), wd, jnp.zeros((width - feat - 1, width), F32)], axis=0
    )
    wfb[...] = block_diag(wide * 0.5).astype(BF16)
    w1b[...] = block_diag(w1.T).astype(BF16)
    w2b[...] = block_diag(w2.T * 0.5).astype(BF16)
    scaled = jnp.concatenate(
        [LOSS_SCALE * pg_ref[...], jnp.zeros((width - feat, rays), F32)], axis=0
    ).T
    sc_ref[...] = scaled
    v_ref[...] = dot_exact(scaled, wide.astype(BF16))
    wd_rows = jnp.broadcast_to(wd, (8, width))
    for ch in range(CHUNKS):
        at = slice(ch * rays_c, (ch + 1) * rays_c)
        count, length = to_samples(count_ref[:, at].astype(F32), step_ref[:, at])
        len_ref[pl.ds(ch * tiles_c, tiles_c), :] = jnp.where(
            (iota((tiles_c, LANES), 1) % per_ray).astype(F32) < count, length, 0.0
        )

    def middle(ch):
        mine = pl.ds(ch * tiles_c, tiles_c)
        logits = lg_ref[mine, :]
        q = q_ref[mine, :]
        length = len_ref[mine, :]
        softplus = jnp.maximum(logits, 0.0) + jnp.log1p(jnp.exp(-jnp.abs(logits)))
        depth_step = softplus * length
        depth_incl = dot_exact(depth_step, upto)
        half_step = jnp.tanh(0.5 * depth_step)
        weights = jnp.exp(depth_step - depth_incl) * (2.0 * half_step / (1.0 + half_step))
        weighted = weights * q
        brick_depth, brick_dot = to_rays(depth_step, weighted)
        ex_ref[ch, 0] = jnp.concatenate([brick_depth, brick_dot, jnp.zeros((6, rays_c), F32)], axis=0)
        c_ref[mine, :] = weights
        q_ref[mine, :] = jnp.exp(-depth_incl) * q - dot_exact(weighted, later)
        len_ref[mine, :] = length * (0.5 + 0.5 * jnp.tanh(0.5 * logits))

    def ex_copy(ch, d):
        return pltpu.make_async_remote_copy(
            src_ref=ex_ref.at[ch, 0],
            dst_ref=ex_ref.at[ch, d],
            send_sem=ex_send.at[ch, d],
            recv_sem=ex_recv.at[ch, d],
            device_id={"brick": lax.rem(my_brick + d, n_brick)},
            device_id_type=MESH,
        )

    def send(ch):
        if ch == 0:
            pl.semaphore_wait(barrier, n_brick + n_ray - 2)
        for d in range(1, n_brick):
            ex_copy(ch, d).start()

    def composite(ch):
        for d in range(1, n_brick):
            ex_copy(ch, d).wait()
        mine = pl.ds(ch * tiles_c, tiles_c)
        there = [ex_ref[ch, lax.rem(my_brick - k + n_brick, n_brick)] for k in range(n_brick)]

        def walk(order, is_past):
            gap = jnp.zeros((1, rays_c), F32)
            seen = jnp.zeros((1, rays_c), F32)
            for k in order:
                past = jnp.where(is_past(k), 1.0, 0.0)
                seen = seen + past * jnp.exp(-gap) * there[k][1:2]
                gap = gap + past * there[k][0:1]
            return gap, seen

        upper_depth, upper_seen = walk(range(n_brick), lambda k: k > my_brick)
        lower_depth, lower_seen = walk(range(n_brick - 1, -1, -1), lambda k: k < my_brick)
        flipped = flip_ref[:, ch * rays_c : (ch + 1) * rays_c] > 0
        through_front = jnp.exp(-jnp.where(flipped, upper_depth, lower_depth))
        behind = jnp.where(flipped, lower_seen, upper_seen)
        brick_depth = ex_ref[ch, 0, 0:1]
        front, brick_grad = to_samples(
            through_front, -through_front * jnp.exp(-brick_depth) * behind
        )
        lg_ref[mine, :] = (front * q_ref[mine, :] + brick_grad) * len_ref[mine, :]
        c_ref[mine, :] = front * c_ref[mine, :]

    def feature_grads(p):
        left, right = [], []
        for k in range(2):
            t = 2 * p + k
            c_hi, c_low = split_two(c_ref[pl.ds(t, 1), :] * group_mask)
            lgm = lg_ref[pl.ds(t, 1), :] * group_mask
            s_hi, s_low = split_two(sc_ref[pl.ds(t * group, group), :])
            left += [c_hi, c_hi, c_low, lgm]
            right += [side(s_hi, k), side(s_low, k), side(s_hi, k), side(unit, k)]
        left = jnp.concatenate(left, axis=0).astype(BF16)
        right = jnp.concatenate(right, axis=0).astype(BF16)
        fg = contract_rows(left, right).astype(BF16)
        put_pair(p1_ref, p, fg)

    def ray_sums(p):
        sums = []
        for k in range(2):
            t = 2 * p + k
            c_hi, c_low = split_two(c_ref[pl.ds(t, 1), :] * group_mask)
            sums += [c_hi, c_low, lg_ref[pl.ds(t, 1), :] * group_mask]
        sums = jnp.concatenate(sums, axis=0).astype(BF16)
        got = jnp.dot(sums, pair_of(h2_ref, p), preferred_element_type=F32)
        dens = jnp.zeros((group, width), F32)
        for k in range(2):
            base = 3 * group * k
            mine = got[:, k * width : (k + 1) * width]
            u_ref[pl.ds((2 * p + k) * group, group), :] = (
                mine[base : base + group] + mine[base + group : base + 2 * group]
            )
            dens = dens + mine[base + 2 * group : base + 3 * group]
        return dens

    def back_two(p):
        h2g = jnp.dot(pair_of(p1_ref, p), wfb[...], preferred_element_type=F32)
        put_pair(p2_ref, p, (h2g * s2_ref[p]).astype(BF16))

    def back_one(p):
        h1g = jnp.dot(pair_of(p2_ref, p), w2b[...], preferred_element_type=F32)
        put_pair(p1_ref, p, (h1g * s1_ref[p]).astype(BF16))

    def finish(p):
        got = jnp.dot(pair_of(p1_ref, p), w1b[...], preferred_element_type=F32).astype(BF16)
        o_ref[pl.ds(p * span, LANES), :] = got[:, :width]
        o_ref[pl.ds(p * span + LANES, LANES), :] = got[:, width:]

    def weight_grad(turned, grads):
        total = None
        for t0 in range(0, tiles, K_TILES):
            left = jnp.concatenate(
                [turned[t] for t in range(t0, t0 + K_TILES)], axis=1
            )
            right = grads[pl.ds(t0, K_TILES)].reshape(K_TILES * LANES, width)
            got = jnp.dot(left, right, preferred_element_type=F32)
            total = got if total is None else total + got
        return total

    share = width // n_ray

    def red_copy(d, first):
        to = lax.rem(my_ray + d, n_ray)
        part = pl.ds(0, 1) if first else pl.ds(1, 2)
        sem = d + n_ray * first
        return pltpu.make_async_remote_copy(
            src_ref=acc.at[part, pl.ds(pl.multiple_of(to * share, share), share), :],
            dst_ref=red_ref.at[d, part],
            send_sem=red_send.at[sem],
            recv_sem=red_recv.at[sem],
            device_id={"ray": to},
            device_id_type=MESH,
        )

    def late_layers(ch):
        first, last = ch * pairs_c, (ch + 1) * pairs_c
        for p in range(first, last + 2, 2):
            for k in (p, p + 1):
                if k < last:
                    second_layer(k)
            for k in (p - 2, p - 1):
                if k >= first:
                    heads(k)

    pieces[0].wait()
    for p in range(pairs_c):
        first_layer(p)
    late_layers(0)
    for ch in range(1, CHUNKS):
        first = ch * pairs_c
        pieces[ch].wait()
        middle(ch - 1)
        for p in range(first, first + HEAD_START):
            first_layer(p)
        send(ch - 1)
        for p in range(first + HEAD_START, first + pairs_c):
            first_layer(p)
        late_layers(ch)
    middle(CHUNKS - 1)
    send(CHUNKS - 1)
    for p in range(pairs):
        turn(p)

    dens = jnp.zeros((group, width), F32)
    for ch in range(CHUNKS):
        first, last = ch * pairs_c, (ch + 1) * pairs_c
        composite(ch)
        if ch > 0:
            for p in range(first - pairs_c, first):
                back_one(p)
        for p in range(first, last):
            feature_grads(p)
        for p in range(first, last):
            dens = dens + ray_sums(p)
        for p in range(first, last):
            back_two(p)
    for p in range(pairs - pairs_c, pairs):
        back_one(p)
    acc[1] = weight_grad(h1t_ref, p2_ref)
    u_hi, u_low = split_two(u_ref[...])
    s_hi, s_low = split_two(sc_ref[...])
    parts = split_three(dens)
    acc[2] = contract_rows(
        jnp.concatenate([u_hi, u_hi, u_low, *parts], axis=0).astype(BF16),
        jnp.concatenate([s_hi, s_low, s_hi, unit, unit, unit], axis=0).astype(BF16),
    )
    for d in range(1, n_ray):
        red_copy(d, 0).start()
    acc[0] = weight_grad(xt_ref, p1_ref)
    for d in range(1, n_ray):
        red_copy(d, 1).start()
    for p in range(pairs):
        finish(p)

    total = acc[:, pl.ds(pl.multiple_of(my_ray * share, share), share), :]
    for d in range(1, n_ray):
        red_copy(d, 0).wait()
        red_copy(d, 1).wait()
        total = total + red_ref[d]
    total = total * (1.0 / LOSS_SCALE)
    g1_ref[0] = total[0]
    g2_ref[0] = total[1]
    g3_ref[0] = total[2][:, :feat]
    g4_ref[...] = total[2].T[feat : feat + 1, :]


def hand_out(*refs):
    held, out, sems = refs[:5], refs[5:10], refs[10]
    copies = [pltpu.make_async_copy(held[i], out[i], sems.at[i]) for i in range(5)]
    for copy in copies:
        copy.start()
    for copy in copies:
        copy.wait()


def solution(mesh):
    n_brick, n_ray = mesh.shape["brick"], mesh.shape["ray"]

    def shards(samples_in, sample_count, step_length, view_flip, pixel_grad, w1, w2, wf, wd):
        rays, _, per_ray, width = samples_in.shape
        feat = pixel_grad.shape[0]
        rows = rays * per_ray
        pairs = rows // (2 * LANES)
        tiles = rows // LANES
        share = width // n_ray
        vmem = pl.BlockSpec(memory_space=pltpu.VMEM)
        hbm = pl.BlockSpec(memory_space=pl.ANY)
        tile_shape = (tiles, LANES, width)
        turned_shape = (tiles, width, LANES)
        outs = pl.pallas_call(
            functools.partial(kernel, n_brick, n_ray, per_ray),
            out_shape=(
                pltpu.VMEM((rows, width), BF16),
                pltpu.VMEM((1, share, width), F32),
                pltpu.VMEM((1, share, width), F32),
                pltpu.VMEM((1, share, feat), F32),
                pltpu.VMEM((1, share), F32),
            ),
            in_specs=[hbm] * 9,
            out_specs=(vmem,) * 5,
            scratch_shapes=[
                pltpu.VMEM((rows, width), BF16),
                pltpu.VMEM((1, rays), jnp.int32),
                pltpu.VMEM((1, rays), F32),
                pltpu.VMEM((1, rays), jnp.int32),
                pltpu.VMEM((feat, rays), F32),
                pltpu.VMEM((1, width, width), BF16),
                pltpu.VMEM((1, width, width), BF16),
                pltpu.VMEM((1, feat, width), BF16),
                pltpu.VMEM((1, width), BF16),
                pltpu.VMEM(turned_shape, BF16),
                pltpu.VMEM(tile_shape, BF16),
                pltpu.VMEM(turned_shape, BF16),
                pltpu.VMEM(tile_shape, BF16),
                pltpu.VMEM(tile_shape, BF16),
                pltpu.VMEM(tile_shape, BF16),
                pltpu.VMEM((pairs, LANES, 2 * width), F32),
                pltpu.VMEM((pairs, LANES, 2 * width), F32),
                pltpu.VMEM((rays, width), F32),
                pltpu.VMEM((rays, width), F32),
                pltpu.VMEM((tiles, LANES), F32),
                pltpu.VMEM((tiles, LANES), F32),
                pltpu.VMEM((tiles, LANES), F32),
                pltpu.VMEM((tiles, LANES), F32),
                pltpu.VMEM((rays, width), F32),
                pltpu.VMEM((2 * width, 2 * width), BF16),
                pltpu.VMEM((2 * width, 2 * width), BF16),
                pltpu.VMEM((2 * width, 2 * width), BF16),
                pltpu.VMEM((2 * width, 2 * width), BF16),
                pltpu.VMEM((2 * width, 2 * width), BF16),
                pltpu.VMEM((3, width, width), F32),
                pltpu.VMEM((CHUNKS, n_brick, 8, rays // CHUNKS), F32),
                pltpu.VMEM((n_ray, 3, share, width), F32),
                pltpu.SemaphoreType.DMA((8,)),
                pltpu.SemaphoreType.DMA((CHUNKS,)),
                pltpu.SemaphoreType.DMA((CHUNKS, n_brick)),
                pltpu.SemaphoreType.DMA((CHUNKS, n_brick)),
                pltpu.SemaphoreType.DMA((2 * n_ray,)),
                pltpu.SemaphoreType.DMA((2 * n_ray,)),
            ],
            compiler_params=pltpu.CompilerParams(
                collective_id=0, has_side_effects=True, vmem_limit_bytes=52 * 1024 * 1024
            ),
        )(
            samples_in.reshape(rows, width),
            sample_count.reshape(1, rays),
            step_length.reshape(1, rays),
            view_flip.reshape(1, rays),
            pixel_grad,
            w1,
            w2,
            jnp.swapaxes(wf, 1, 2),
            wd,
        )
        outs = pl.pallas_call(
            hand_out,
            out_shape=tuple(jax.ShapeDtypeStruct(o.shape, o.dtype) for o in outs),
            in_specs=[vmem] * 5,
            out_specs=(hbm,) * 5,
            scratch_shapes=[pltpu.SemaphoreType.DMA((5,))],
            compiler_params=pltpu.CompilerParams(vmem_limit_bytes=4 * 1024 * 1024),
        )(*[pltpu.with_memory_space_constraint(o, pltpu.VMEM) for o in outs])
        return (outs[0].reshape(samples_in.shape),) + tuple(outs[1:])

    placed = (
        P(("groups", "ray"), "brick", None, None),
        P(("groups", "ray"), "brick"),
        P(("groups", "ray")),
        P(("groups", "ray")),
        P(None, ("groups", "ray")),
        P("brick", None, None),
        P("brick", None, None),
        P("brick", None, None),
        P("brick", None),
    )
    return jax.shard_map(
        shards,
        mesh=mesh,
        in_specs=placed,
        out_specs=(
            P(("groups", "ray"), "brick", None, None),
            P(("groups", "brick"), "ray", None),
            P(("groups", "brick"), "ray", None),
            P(("groups", "brick"), "ray", None),
            P(("groups", "brick"), "ray"),
        ),
        check_vma=False,
    )
```

```python
import functools

import jax
import jax.numpy as jnp
from jax import lax
from jax.experimental import pallas as pl
from jax.experimental.pallas import tpu as pltpu
from jax.sharding import PartitionSpec as P

LOSS_SCALE = 1024.0
LANES = 256
CHUNKS = 2
K_TILES = 8
HEAD_START = 0
F32 = jnp.float32
BF16 = jnp.bfloat16
MESH = pl.DeviceIdType.MESH


def iota(shape, dim):
    return lax.broadcasted_iota(jnp.int32, shape, dim)


def split_two(v):
    hi = v.astype(BF16).astype(F32)
    return hi, v - hi


def split_three(v):
    hi, rest = split_two(v)
    mid, low = split_two(rest)
    return hi, mid, low


def dot_exact(v, m):
    rows = v.shape[0]
    out = jnp.dot(
        jnp.concatenate(split_three(v), axis=0).astype(BF16), m, preferred_element_type=F32
    )
    return out[:rows] + out[rows : 2 * rows] + out[2 * rows :]


def contract_rows(left, right):
    return lax.dot_general(left, right, (((0,), (0,)), ((), ())), preferred_element_type=F32)


def block_diag(w):
    z = jnp.zeros_like(w)
    return jnp.concatenate(
        [jnp.concatenate([w, z], axis=1), jnp.concatenate([z, w], axis=1)], axis=0
    )


def side(v, right):
    z = jnp.zeros_like(v)
    return jnp.concatenate([z, v] if right else [v, z], axis=1)


def silu_pair(half):
    a = 1.0 + jnp.tanh(half)
    return half * a, a


def slope_of(gate_ref, act_ref, p):
    a = gate_ref[p]
    return a + act_ref[p] * (2.0 - a)


def kernel(
    n_brick,
    n_ray,
    per_ray,
    x_hbm,
    count_hbm,
    step_hbm,
    flip_hbm,
    pg_hbm,
    w1_hbm,
    w2_hbm,
    wf_hbm,
    wd_hbm,
    o_ref,
    g1_ref,
    g2_ref,
    g3_ref,
    g4_ref,
    x_ref,
    count_ref,
    step_ref,
    flip_ref,
    pg_ref,
    w1_ref,
    w2_ref,
    wf_ref,
    wd_ref,
    xt_ref,
    h1_ref,
    h1t_ref,
    h2_ref,
    p1_ref,
    p2_ref,
    s1_ref,
    s2_ref,
    f1_ref,
    f2_ref,
    v_ref,
    sc_ref,
    q_ref,
    lg_ref,
    len_ref,
    c_ref,
    u_ref,
    w1f,
    w2f,
    w1b,
    w2b,
    wfb,
    acc,
    ex_ref,
    red_ref,
    in_sem,
    x_sem,
    ex_send,
    ex_recv,
    red_send,
    red_recv,
):
    rows, width = x_ref.shape
    feat, rays = pg_ref.shape
    group = LANES // per_ray
    tiles = rows // LANES
    pairs = tiles // 2
    span = 2 * LANES
    half = LANES // 2

    small = [
        pltpu.make_async_copy(src, dst, in_sem.at[i])
        for i, (src, dst) in enumerate(
            (
                (w1_hbm, w1_ref),
                (w2_hbm, w2_ref),
                (wf_hbm, wf_ref),
                (wd_hbm, wd_ref),
                (pg_hbm, pg_ref),
                (count_hbm, count_ref),
                (step_hbm, step_ref),
                (flip_hbm, flip_ref),
            )
        )
    ]
    piece = rows // CHUNKS
    pieces = [
        pltpu.make_async_copy(
            x_hbm.at[pl.ds(i * piece, piece)], x_ref.at[pl.ds(i * piece, piece)], x_sem.at[i]
        )
        for i in range(CHUNKS)
    ]
    small[0].start()
    pieces[0].start()
    for copy in small[1:] + pieces[1:]:
        copy.start()

    my_brick = lax.axis_index("brick")
    my_ray = lax.axis_index("ray")
    barrier = pltpu.get_barrier_semaphore()
    for d in range(1, n_brick):
        pl.semaphore_signal(
            barrier, inc=1, device_id={"brick": lax.rem(my_brick + d, n_brick)}, device_id_type=MESH
        )
    for d in range(1, n_ray):
        pl.semaphore_signal(
            barrier, inc=1, device_id={"ray": lax.rem(my_ray + d, n_ray)}, device_id_type=MESH
        )

    group_mask = (iota((group, LANES), 0) == iota((group, LANES), 1) // per_ray).astype(F32)
    unit = (iota((8, width), 1) == feat).astype(F32)
    rays_c = rays // CHUNKS
    tiles_c = tiles // CHUNKS
    pairs_c = pairs // CHUNKS
    spread = (iota((rays_c, LANES), 0) % group == iota((rays_c, LANES), 1) // per_ray).astype(BF16)
    gather = (iota((LANES, rays_c), 1) % group == iota((LANES, rays_c), 0) // per_ray).astype(BF16)
    owner = (iota((tiles_c, rays_c), 1) // group == iota((tiles_c, rays_c), 0)).astype(F32)
    from_s, to_s = iota((LANES, LANES), 0), iota((LANES, LANES), 1)
    same = from_s // per_ray == to_s // per_ray
    upto = (same & (from_s <= to_s)).astype(BF16)
    later = (same & (from_s > to_s)).astype(BF16)

    def to_samples(*ray_rows):
        out = dot_exact(jnp.concatenate([owner * r for r in ray_rows], axis=0), spread)
        return [out[i * tiles_c : (i + 1) * tiles_c] for i in range(len(ray_rows))]

    def to_rays(*sample_values):
        out = dot_exact(jnp.concatenate(sample_values, axis=0), gather)
        return [
            jnp.sum(out[i * tiles_c : (i + 1) * tiles_c] * owner, axis=0, keepdims=True)
            for i in range(len(sample_values))
        ]

    for copy in small:
        copy.wait()
    w1 = w1_ref[0].astype(F32)
    w1f[...] = block_diag(w1 * 0.5).astype(BF16)

    def pair_of(ref, p):
        return jnp.concatenate([ref[2 * p], ref[2 * p + 1]], axis=1)

    def put_pair(ref, p, v):
        ref[2 * p] = v[:, :width]
        ref[2 * p + 1] = v[:, width:]

    def put_turned(ref, p, v):
        for k in range(2):
            ref[2 * p + k] = v[:, k * width : (k + 1) * width].T

    def x_pair(p):
        return jnp.concatenate(
            [x_ref[pl.ds(p * span, LANES), :], x_ref[pl.ds(p * span + LANES, LANES), :]], axis=1
        )

    def first_layer(p):
        h1, s1 = silu_pair(jnp.dot(x_pair(p), w1f[...], preferred_element_type=F32))
        put_pair(h1_ref, p, h1.astype(BF16))
        s1_ref[p] = s1
        f1_ref[p] = h1

    def turn(p):
        put_turned(h1t_ref, p, pair_of(h1_ref, p))
        put_turned(xt_ref, p, x_pair(p))

    def second_layer(p):
        h2, s2 = silu_pair(jnp.dot(pair_of(h1_ref, p), w2f[...], preferred_element_type=F32))
        put_pair(h2_ref, p, h2.astype(BF16))
        s2_ref[p] = s2
        f2_ref[p] = h2

    def heads(p):
        left = []
        for k in range(2):
            hi, low = split_two(v_ref[pl.ds((2 * p + k) * group, group), :])
            left += [side(hi, k), side(low, k), side(wd_rows, k)]
        left = jnp.concatenate(left, axis=0).astype(BF16)
        got = lax.dot_general(
            left, pair_of(h2_ref, p), (((1,), (1,)), ((), ())), preferred_element_type=F32
        )
        for k in range(2):
            base = k * (2 * group + 8)
            dots = got[base : base + group] + got[base + group : base + 2 * group]
            q_ref[pl.ds(2 * p + k, 1), :] = jnp.sum(dots * group_mask, axis=0, keepdims=True)
            lg_ref[pl.ds(2 * p + k, 1), :] = got[base + 2 * group : base + 2 * group + 1]

    w2 = w2_ref[0].astype(F32)
    wd = wd_ref[...].astype(F32)
    w2f[...] = block_diag(w2 * 0.5).astype(BF16)
    wide = jnp.concatenate(
        [wf_ref[0].astype(F32), wd, jnp.zeros((width - feat - 1, width), F32)], axis=0
    )
    wfb[...] = block_diag(wide * 0.5).astype(BF16)
    w1b[...] = block_diag(w1.T).astype(BF16)
    w2b[...] = block_diag(w2.T * 0.5).astype(BF16)
    scaled = jnp.concatenate(
        [LOSS_SCALE * pg_ref[...], jnp.zeros((width - feat, rays), F32)], axis=0
    ).T
    sc_ref[...] = scaled
    v_ref[...] = dot_exact(scaled, wide.astype(BF16))
    wd_rows = jnp.broadcast_to(wd, (8, width))
    for ch in range(CHUNKS):
        at = slice(ch * rays_c, (ch + 1) * rays_c)
        count, length = to_samples(count_ref[:, at].astype(F32), step_ref[:, at])
        len_ref[pl.ds(ch * tiles_c, tiles_c), :] = jnp.where(
            (iota((tiles_c, LANES), 1) % per_ray).astype(F32) < count, length, 0.0
        )

    def middle(ch):
        mine = pl.ds(ch * tiles_c, tiles_c)
        logits = lg_ref[mine, :]
        q = q_ref[mine, :]
        length = len_ref[mine, :]
        softplus = jnp.maximum(logits, 0.0) + jnp.log1p(jnp.exp(-jnp.abs(logits)))
        depth_step = softplus * length
        depth_incl = dot_exact(depth_step, upto)
        half_step = jnp.tanh(0.5 * depth_step)
        weights = jnp.exp(depth_step - depth_incl) * (2.0 * half_step / (1.0 + half_step))
        weighted = weights * q
        brick_depth, brick_dot = to_rays(depth_step, weighted)
        ex_ref[ch, 0] = jnp.concatenate([brick_depth, brick_dot, jnp.zeros((6, rays_c), F32)], axis=0)
        c_ref[mine, :] = weights
        q_ref[mine, :] = jnp.exp(-depth_incl) * q - dot_exact(weighted, later)
        len_ref[mine, :] = length * (0.5 + 0.5 * jnp.tanh(0.5 * logits))

    def ex_copy(ch, d):
        return pltpu.make_async_remote_copy(
            src_ref=ex_ref.at[ch, 0],
            dst_ref=ex_ref.at[ch, d],
            send_sem=ex_send.at[ch, d],
            recv_sem=ex_recv.at[ch, d],
            device_id={"brick": lax.rem(my_brick + d, n_brick)},
            device_id_type=MESH,
        )

    def send(ch):
        if ch == 0:
            pl.semaphore_wait(barrier, n_brick + n_ray - 2)
        for d in range(1, n_brick):
            ex_copy(ch, d).start()

    def composite(ch):
        for d in range(1, n_brick):
            ex_copy(ch, d).wait()
        mine = pl.ds(ch * tiles_c, tiles_c)
        there = [ex_ref[ch, lax.rem(my_brick - k + n_brick, n_brick)] for k in range(n_brick)]

        def walk(order, is_past):
            gap = jnp.zeros((1, rays_c), F32)
            seen = jnp.zeros((1, rays_c), F32)
            for k in order:
                past = jnp.where(is_past(k), 1.0, 0.0)
                seen = seen + past * jnp.exp(-gap) * there[k][1:2]
                gap = gap + past * there[k][0:1]
            return gap, seen

        upper_depth, upper_seen = walk(range(n_brick), lambda k: k > my_brick)
        lower_depth, lower_seen = walk(range(n_brick - 1, -1, -1), lambda k: k < my_brick)
        flipped = flip_ref[:, ch * rays_c : (ch + 1) * rays_c] > 0
        through_front = jnp.exp(-jnp.where(flipped, upper_depth, lower_depth))
        behind = jnp.where(flipped, lower_seen, upper_seen)
        brick_depth = ex_ref[ch, 0, 0:1]
        front, brick_grad = to_samples(
            through_front, -through_front * jnp.exp(-brick_depth) * behind
        )
        lg_ref[mine, :] = (front * q_ref[mine, :] + brick_grad) * len_ref[mine, :]
        c_ref[mine, :] = front * c_ref[mine, :]

    def feature_grads(p):
        left, right = [], []
        for k in range(2):
            t = 2 * p + k
            c_hi, c_low = split_two(c_ref[pl.ds(t, 1), :] * group_mask)
            lgm = lg_ref[pl.ds(t, 1), :] * group_mask
            s_hi, s_low = split_two(sc_ref[pl.ds(t * group, group), :])
            left += [c_hi, c_hi, c_low, lgm]
            right += [side(s_hi, k), side(s_low, k), side(s_hi, k), side(unit, k)]
        left = jnp.concatenate(left, axis=0).astype(BF16)
        right = jnp.concatenate(right, axis=0).astype(BF16)
        fg = contract_rows(left, right).astype(BF16)
        put_pair(p1_ref, p, fg)

    def ray_sums(p):
        sums = []
        for k in range(2):
            t = 2 * p + k
            c_hi, c_low = split_two(c_ref[pl.ds(t, 1), :] * group_mask)
            sums += [c_hi, c_low, lg_ref[pl.ds(t, 1), :] * group_mask]
        sums = jnp.concatenate(sums, axis=0).astype(BF16)
        got = jnp.dot(sums, pair_of(h2_ref, p), preferred_element_type=F32)
        dens = jnp.zeros((group, width), F32)
        for k in range(2):
            base = 3 * group * k
            mine = got[:, k * width : (k + 1) * width]
            u_ref[pl.ds((2 * p + k) * group, group), :] = (
                mine[base : base + group] + mine[base + group : base + 2 * group]
            )
            dens = dens + mine[base + 2 * group : base + 3 * group]
        return dens

    def back_two(p):
        h2g = jnp.dot(pair_of(p1_ref, p), wfb[...], preferred_element_type=F32)
        put_pair(p2_ref, p, (h2g * slope_of(s2_ref, f2_ref, p)).astype(BF16))

    def back_one(p):
        h1g = jnp.dot(pair_of(p2_ref, p), w2b[...], preferred_element_type=F32)
        put_pair(p1_ref, p, (h1g * slope_of(s1_ref, f1_ref, p)).astype(BF16))

    def finish(p):
        got = jnp.dot(pair_of(p1_ref, p), w1b[...], preferred_element_type=F32).astype(BF16)
        o_ref[pl.ds(p * span, LANES), :] = got[:, :width]
        o_ref[pl.ds(p * span + LANES, LANES), :] = got[:, width:]

    def weight_grad(turned, grads, ch):
        total = None
        for t0 in range(ch * tiles_c, (ch + 1) * tiles_c, K_TILES):
            left = jnp.concatenate(
                [turned[t] for t in range(t0, t0 + K_TILES)], axis=1
            )
            right = grads[pl.ds(t0, K_TILES)].reshape(K_TILES * LANES, width)
            got = jnp.dot(left, right, preferred_element_type=F32)
            total = got if total is None else total + got
        return total

    share = width // n_ray

    def red_copy(d, m):
        to = lax.rem(my_ray + d, n_ray)
        return pltpu.make_async_remote_copy(
            src_ref=acc.at[pl.ds(m, 1), pl.ds(pl.multiple_of(to * share, share), share), :],
            dst_ref=red_ref.at[d, pl.ds(m, 1)],
            send_sem=red_send.at[m * n_ray + d],
            recv_sem=red_recv.at[m * n_ray + d],
            device_id={"ray": to},
            device_id_type=MESH,
        )

    partners = sorted(range(1, n_ray), key=lambda d: abs(d - n_ray // 2))

    def add_grad(m, value, ch):
        acc[m] = value if ch == 0 else acc[m] + value

    def late_layers(ch):
        first, last = ch * pairs_c, (ch + 1) * pairs_c
        for p in range(first, last + 2, 2):
            for k in (p, p + 1):
                if k < last:
                    second_layer(k)
            for k in (p - 2, p - 1):
                if k >= first:
                    heads(k)

    pieces[0].wait()
    for p in range(pairs_c):
        first_layer(p)
    late_layers(0)
    for ch in range(1, CHUNKS):
        first = ch * pairs_c
        pieces[ch].wait()
        middle(ch - 1)
        for p in range(first, first + HEAD_START):
            first_layer(p)
        send(ch - 1)
        for p in range(first + HEAD_START, first + pairs_c):
            first_layer(p)
        late_layers(ch)
    middle(CHUNKS - 1)
    send(CHUNKS - 1)
    for p in range(pairs):
        turn(p)

    dens = jnp.zeros((group, width), F32)
    for ch in range(CHUNKS):
        first, last = ch * pairs_c, (ch + 1) * pairs_c
        composite(ch)
        if ch > 0:
            add_grad(0, weight_grad(xt_ref, p1_ref, ch - 1), ch - 1)
        for p in range(first, last):
            feature_grads(p)
        for p in range(first, last):
            dens = dens + ray_sums(p)
        for p in range(first, last):
            back_two(p)
        if ch < CHUNKS - 1:
            for p in range(first, last):
                back_one(p)
            add_grad(1, weight_grad(h1t_ref, p2_ref, ch), ch)
    u_hi, u_low = split_two(u_ref[...])
    s_hi, s_low = split_two(sc_ref[...])
    left = jnp.concatenate([u_hi, u_hi, u_low, *split_three(dens)], axis=0)
    right = jnp.concatenate([s_hi, s_low, s_hi, unit, unit, unit], axis=0)
    acc[2] = contract_rows(left.astype(BF16), right.astype(BF16))
    add_grad(1, weight_grad(h1t_ref, p2_ref, CHUNKS - 1), CHUNKS - 1)
    for d in partners:
        red_copy(d, 1).start()
        red_copy(d, 2).start()
    for p in range(pairs - pairs_c, pairs):
        back_one(p)
    add_grad(0, weight_grad(xt_ref, p1_ref, CHUNKS - 1), CHUNKS - 1)
    for d in partners:
        red_copy(d, 0).start()
    for p in range(pairs):
        finish(p)

    def reduced(m):
        total = acc[m, pl.ds(pl.multiple_of(my_ray * share, share), share), :]
        for d in partners:
            red_copy(d, m).wait()
            total = total + red_ref[d, m]
        return total * (1.0 / LOSS_SCALE)

    both = reduced(2)
    g3_ref[0] = both[:, :feat]
    g4_ref[...] = both.T[feat : feat + 1, :]
    g2_ref[0] = reduced(1)
    g1_ref[0] = reduced(0)


def hand_out(*refs):
    held, out, sems = refs[:5], refs[5:10], refs[10]
    copies = [pltpu.make_async_copy(held[i], out[i], sems.at[i]) for i in range(5)]
    for copy in copies:
        copy.start()
    for copy in copies:
        copy.wait()


def solution(mesh):
    n_brick, n_ray = mesh.shape["brick"], mesh.shape["ray"]

    def shards(samples_in, sample_count, step_length, view_flip, pixel_grad, w1, w2, wf, wd):
        rays, _, per_ray, width = samples_in.shape
        feat = pixel_grad.shape[0]
        rows = rays * per_ray
        pairs = rows // (2 * LANES)
        tiles = rows // LANES
        share = width // n_ray
        vmem = pl.BlockSpec(memory_space=pltpu.VMEM)
        hbm = pl.BlockSpec(memory_space=pl.ANY)
        tile_shape = (tiles, LANES, width)
        turned_shape = (tiles, width, LANES)
        outs = pl.pallas_call(
            functools.partial(kernel, n_brick, n_ray, per_ray),
            out_shape=(
                pltpu.VMEM((rows, width), BF16),
                pltpu.VMEM((1, share, width), F32),
                pltpu.VMEM((1, share, width), F32),
                pltpu.VMEM((1, share, feat), F32),
                pltpu.VMEM((1, share), F32),
            ),
            in_specs=[hbm] * 9,
            out_specs=(vmem,) * 5,
            scratch_shapes=[
                pltpu.VMEM((rows, width), BF16),
                pltpu.VMEM((1, rays), jnp.int32),
                pltpu.VMEM((1, rays), F32),
                pltpu.VMEM((1, rays), jnp.int32),
                pltpu.VMEM((feat, rays), F32),
                pltpu.VMEM((1, width, width), BF16),
                pltpu.VMEM((1, width, width), BF16),
                pltpu.VMEM((1, feat, width), BF16),
                pltpu.VMEM((1, width), BF16),
                pltpu.VMEM(turned_shape, BF16),
                pltpu.VMEM(tile_shape, BF16),
                pltpu.VMEM(turned_shape, BF16),
                pltpu.VMEM(tile_shape, BF16),
                pltpu.VMEM(tile_shape, BF16),
                pltpu.VMEM(tile_shape, BF16),
                pltpu.VMEM((pairs, LANES, 2 * width), F32),
                pltpu.VMEM((pairs, LANES, 2 * width), F32),
                pltpu.VMEM((pairs, LANES, 2 * width), F32),
                pltpu.VMEM((pairs, LANES, 2 * width), F32),
                pltpu.VMEM((rays, width), F32),
                pltpu.VMEM((rays, width), F32),
                pltpu.VMEM((tiles, LANES), F32),
                pltpu.VMEM((tiles, LANES), F32),
                pltpu.VMEM((tiles, LANES), F32),
                pltpu.VMEM((tiles, LANES), F32),
                pltpu.VMEM((rays, width), F32),
                pltpu.VMEM((2 * width, 2 * width), BF16),
                pltpu.VMEM((2 * width, 2 * width), BF16),
                pltpu.VMEM((2 * width, 2 * width), BF16),
                pltpu.VMEM((2 * width, 2 * width), BF16),
                pltpu.VMEM((2 * width, 2 * width), BF16),
                pltpu.VMEM((3, width, width), F32),
                pltpu.VMEM((CHUNKS, n_brick, 8, rays // CHUNKS), F32),
                pltpu.VMEM((n_ray, 3, share, width), F32),
                pltpu.SemaphoreType.DMA((8,)),
                pltpu.SemaphoreType.DMA((CHUNKS,)),
                pltpu.SemaphoreType.DMA((CHUNKS, n_brick)),
                pltpu.SemaphoreType.DMA((CHUNKS, n_brick)),
                pltpu.SemaphoreType.DMA((3 * n_ray,)),
                pltpu.SemaphoreType.DMA((3 * n_ray,)),
            ],
            compiler_params=pltpu.CompilerParams(
                collective_id=0, has_side_effects=True, vmem_limit_bytes=52 * 1024 * 1024
            ),
        )(
            samples_in.reshape(rows, width),
            sample_count.reshape(1, rays),
            step_length.reshape(1, rays),
            view_flip.reshape(1, rays),
            pixel_grad,
            w1,
            w2,
            jnp.swapaxes(wf, 1, 2),
            wd,
        )
        outs = pl.pallas_call(
            hand_out,
            out_shape=tuple(jax.ShapeDtypeStruct(o.shape, o.dtype) for o in outs),
            in_specs=[vmem] * 5,
            out_specs=(hbm,) * 5,
            scratch_shapes=[pltpu.SemaphoreType.DMA((5,))],
            compiler_params=pltpu.CompilerParams(vmem_limit_bytes=4 * 1024 * 1024),
        )(*[pltpu.with_memory_space_constraint(o, pltpu.VMEM) for o in outs])
        return (outs[0].reshape(samples_in.shape),) + tuple(outs[1:])

    placed = (
        P(("groups", "ray"), "brick", None, None),
        P(("groups", "ray"), "brick"),
        P(("groups", "ray")),
        P(("groups", "ray")),
        P(None, ("groups", "ray")),
        P("brick", None, None),
        P("brick", None, None),
        P("brick", None, None),
        P("brick", None),
    )
    return jax.shard_map(
        shards,
        mesh=mesh,
        in_specs=placed,
        out_specs=(
            P(("groups", "ray"), "brick", None, None),
            P(("groups", "brick"), "ray", None),
            P(("groups", "brick"), "ray", None),
            P(("groups", "brick"), "ray", None),
            P(("groups", "brick"), "ray"),
        ),
        check_vma=False,
    )
```

```python
import functools

import jax
import jax.numpy as jnp
from jax import lax
from jax.experimental import pallas as pl
from jax.experimental.pallas import tpu as pltpu
from jax.sharding import PartitionSpec as P

LOSS_SCALE = 1024.0
LANES = 256
CHUNKS = 2
K_TILES = 16
HEAD_START = 0
EARLY_PAIRS = 2
F32 = jnp.float32
BF16 = jnp.bfloat16
MESH = pl.DeviceIdType.MESH


def iota(shape, dim):
    return lax.broadcasted_iota(jnp.int32, shape, dim)


def split_two(v):
    hi = v.astype(BF16).astype(F32)
    return hi, v - hi


def split_three(v):
    hi, rest = split_two(v)
    mid, low = split_two(rest)
    return hi, mid, low


def dot_exact(v, m):
    rows = v.shape[0]
    out = jnp.dot(
        jnp.concatenate(split_three(v), axis=0).astype(BF16), m, preferred_element_type=F32
    )
    return out[:rows] + out[rows : 2 * rows] + out[2 * rows :]


def contract_rows(left, right):
    return lax.dot_general(left, right, (((0,), (0,)), ((), ())), preferred_element_type=F32)


def block_diag(w):
    z = jnp.zeros_like(w)
    return jnp.concatenate(
        [jnp.concatenate([w, z], axis=1), jnp.concatenate([z, w], axis=1)], axis=0
    )


def side(v, right):
    z = jnp.zeros_like(v)
    return jnp.concatenate([z, v] if right else [v, z], axis=1)


def silu_pair(half):
    a = 1.0 + jnp.tanh(half)
    return half * a, a


def slope_of(gate_ref, act_ref, p):
    a = gate_ref[p]
    return a + act_ref[p] * (2.0 - a)


def kernel(
    n_brick,
    n_ray,
    per_ray,
    x_hbm,
    count_hbm,
    step_hbm,
    flip_hbm,
    pg_hbm,
    w1_hbm,
    w2_hbm,
    wf_hbm,
    wd_hbm,
    o_ref,
    g1_ref,
    g2_ref,
    g3_ref,
    g4_ref,
    x_ref,
    count_ref,
    step_ref,
    flip_ref,
    pg_ref,
    w1_ref,
    w2_ref,
    wf_ref,
    wd_ref,
    xt_ref,
    h1_ref,
    h1t_ref,
    h2_ref,
    p1_ref,
    p2_ref,
    s1_ref,
    s2_ref,
    f1_ref,
    v_ref,
    sc_ref,
    q_ref,
    lg_ref,
    len_ref,
    c_ref,
    u_ref,
    w1f,
    w2f,
    w1b,
    w2b,
    wfb,
    acc,
    ex_ref,
    red_ref,
    in_sem,
    x_sem,
    ex_send,
    ex_recv,
    red_send,
    red_recv,
):
    rows, width = x_ref.shape
    feat, rays = pg_ref.shape
    group = LANES // per_ray
    tiles = rows // LANES
    pairs = tiles // 2
    span = 2 * LANES
    half = LANES // 2

    small = [
        pltpu.make_async_copy(src, dst, in_sem.at[i])
        for i, (src, dst) in enumerate(
            (
                (w1_hbm, w1_ref),
                (w2_hbm, w2_ref),
                (wf_hbm, wf_ref),
                (wd_hbm, wd_ref),
                (pg_hbm, pg_ref),
                (count_hbm, count_ref),
                (step_hbm, step_ref),
                (flip_hbm, flip_ref),
            )
        )
    ]
    chunk_rows = rows // CHUNKS
    cuts = [0, EARLY_PAIRS * span] + [(i + 1) * chunk_rows for i in range(CHUNKS)]
    pieces = [
        pltpu.make_async_copy(
            x_hbm.at[pl.ds(lo, hi - lo)], x_ref.at[pl.ds(lo, hi - lo)], x_sem.at[i]
        )
        for i, (lo, hi) in enumerate(zip(cuts, cuts[1:]))
    ]
    small[0].start()
    pieces[0].start()
    for copy in small[1:] + pieces[1:]:
        copy.start()

    my_brick = lax.axis_index("brick")
    my_ray = lax.axis_index("ray")
    barrier = pltpu.get_barrier_semaphore()
    for d in range(1, n_brick):
        pl.semaphore_signal(
            barrier, inc=1, device_id={"brick": lax.rem(my_brick + d, n_brick)}, device_id_type=MESH
        )
    for d in range(1, n_ray):
        pl.semaphore_signal(
            barrier, inc=1, device_id={"ray": lax.rem(my_ray + d, n_ray)}, device_id_type=MESH
        )

    group_mask = (iota((group, LANES), 0) == iota((group, LANES), 1) // per_ray).astype(F32)
    unit = (iota((8, width), 1) == feat).astype(F32)
    rays_c = rays // CHUNKS
    tiles_c = tiles // CHUNKS
    pairs_c = pairs // CHUNKS
    spread = (iota((rays_c, LANES), 0) % group == iota((rays_c, LANES), 1) // per_ray).astype(BF16)
    gather = (iota((LANES, rays_c), 1) % group == iota((LANES, rays_c), 0) // per_ray).astype(BF16)
    owner = (iota((tiles_c, rays_c), 1) // group == iota((tiles_c, rays_c), 0)).astype(F32)
    from_s, to_s = iota((LANES, LANES), 0), iota((LANES, LANES), 1)
    same = from_s // per_ray == to_s // per_ray
    upto = (same & (from_s <= to_s)).astype(BF16)
    later = (same & (from_s > to_s)).astype(BF16)

    def to_samples(*ray_rows):
        out = dot_exact(jnp.concatenate([owner * r for r in ray_rows], axis=0), spread)
        return [out[i * tiles_c : (i + 1) * tiles_c] for i in range(len(ray_rows))]

    def to_rays(*sample_values):
        out = dot_exact(jnp.concatenate(sample_values, axis=0), gather)
        return [
            jnp.sum(out[i * tiles_c : (i + 1) * tiles_c] * owner, axis=0, keepdims=True)
            for i in range(len(sample_values))
        ]

    for copy in small + pieces[:1]:
        copy.wait()
    w1 = w1_ref[0].astype(F32)
    w1f[...] = block_diag(w1 * 0.5).astype(BF16)

    def pair_of(ref, p):
        return jnp.concatenate([ref[2 * p], ref[2 * p + 1]], axis=1)

    def put_pair(ref, p, v):
        ref[2 * p] = v[:, :width]
        ref[2 * p + 1] = v[:, width:]

    def put_turned(ref, p, v):
        for k in range(2):
            ref[2 * p + k] = v[:, k * width : (k + 1) * width].T

    def x_pair(p):
        return jnp.concatenate(
            [x_ref[pl.ds(p * span, LANES), :], x_ref[pl.ds(p * span + LANES, LANES), :]], axis=1
        )

    def first_layer(p):
        h1, s1 = silu_pair(jnp.dot(x_pair(p), w1f[...], preferred_element_type=F32))
        put_pair(h1_ref, p, h1.astype(BF16))
        s1_ref[p] = s1
        f1_ref[p] = h1

    def turn(p):
        put_turned(h1t_ref, p, pair_of(h1_ref, p))
        put_turned(xt_ref, p, x_pair(p))

    def second_layer(p):
        h2, s2 = silu_pair(jnp.dot(pair_of(h1_ref, p), w2f[...], preferred_element_type=F32))
        put_pair(h2_ref, p, h2.astype(BF16))
        s2_ref[p] = s2 + h2 * (2.0 - s2)

    def heads(p):
        left = []
        for k in range(2):
            hi, low = split_two(v_ref[pl.ds((2 * p + k) * group, group), :])
            left += [side(hi, k), side(low, k), side(wd_rows, k)]
        left = jnp.concatenate(left, axis=0).astype(BF16)
        got = lax.dot_general(
            left, pair_of(h2_ref, p), (((1,), (1,)), ((), ())), preferred_element_type=F32
        )
        for k in range(2):
            base = k * (2 * group + 8)
            dots = got[base : base + group] + got[base + group : base + 2 * group]
            q_ref[pl.ds(2 * p + k, 1), :] = jnp.sum(dots * group_mask, axis=0, keepdims=True)
            lg_ref[pl.ds(2 * p + k, 1), :] = got[base + 2 * group : base + 2 * group + 1]

    w2 = w2_ref[0].astype(F32)
    wd = wd_ref[...].astype(F32)
    w2f[...] = block_diag(w2 * 0.5).astype(BF16)
    wide = jnp.concatenate(
        [wf_ref[0].astype(F32), wd, jnp.zeros((width - feat - 1, width), F32)], axis=0
    )
    wfb[...] = block_diag(wide * 0.5).astype(BF16)
    w1b[...] = block_diag(w1.T).astype(BF16)
    w2b[...] = block_diag(w2.T * 0.5).astype(BF16)
    scaled = jnp.concatenate(
        [LOSS_SCALE * pg_ref[...], jnp.zeros((width - feat, rays), F32)], axis=0
    ).T
    sc_ref[...] = scaled
    v_ref[...] = dot_exact(scaled, wide.astype(BF16))
    wd_rows = jnp.broadcast_to(wd, (8, width))
    for ch in range(CHUNKS):
        at = slice(ch * rays_c, (ch + 1) * rays_c)
        count, length = to_samples(count_ref[:, at].astype(F32), step_ref[:, at])
        len_ref[pl.ds(ch * tiles_c, tiles_c), :] = jnp.where(
            (iota((tiles_c, LANES), 1) % per_ray).astype(F32) < count, length, 0.0
        )

    def middle(ch):
        mine = pl.ds(ch * tiles_c, tiles_c)
        logits = lg_ref[mine, :]
        q = q_ref[mine, :]
        length = len_ref[mine, :]
        softplus = jnp.maximum(logits, 0.0) + jnp.log1p(jnp.exp(-jnp.abs(logits)))
        depth_step = softplus * length
        depth_incl = dot_exact(depth_step, upto)
        half_step = jnp.tanh(0.5 * depth_step)
        weights = jnp.exp(depth_step - depth_incl) * (2.0 * half_step / (1.0 + half_step))
        weighted = weights * q
        brick_depth, brick_dot = to_rays(depth_step, weighted)
        ex_ref[ch, 0] = jnp.concatenate([brick_depth, brick_dot, jnp.zeros((6, rays_c), F32)], axis=0)
        c_ref[mine, :] = weights
        q_ref[mine, :] = jnp.exp(-depth_incl) * q - dot_exact(weighted, later)
        len_ref[mine, :] = length * (0.5 + 0.5 * jnp.tanh(0.5 * logits))

    def ex_copy(ch, d):
        return pltpu.make_async_remote_copy(
            src_ref=ex_ref.at[ch, 0],
            dst_ref=ex_ref.at[ch, d],
            send_sem=ex_send.at[ch, d],
            recv_sem=ex_recv.at[ch, d],
            device_id={"brick": lax.rem(my_brick + d, n_brick)},
            device_id_type=MESH,
        )

    def send(ch):
        if ch == 0:
            pl.semaphore_wait(barrier, n_brick + n_ray - 2)
        for d in range(1, n_brick):
            ex_copy(ch, d).start()

    def composite(ch):
        for d in range(1, n_brick):
            ex_copy(ch, d).wait()
        mine = pl.ds(ch * tiles_c, tiles_c)
        there = [ex_ref[ch, lax.rem(my_brick - k + n_brick, n_brick)] for k in range(n_brick)]

        def walk(order, is_past):
            gap = jnp.zeros((1, rays_c), F32)
            seen = jnp.zeros((1, rays_c), F32)
            for k in order:
                past = jnp.where(is_past(k), 1.0, 0.0)
                seen = seen + past * jnp.exp(-gap) * there[k][1:2]
                gap = gap + past * there[k][0:1]
            return gap, seen

        upper_depth, upper_seen = walk(range(n_brick), lambda k: k > my_brick)
        lower_depth, lower_seen = walk(range(n_brick - 1, -1, -1), lambda k: k < my_brick)
        flipped = flip_ref[:, ch * rays_c : (ch + 1) * rays_c] > 0
        through_front = jnp.exp(-jnp.where(flipped, upper_depth, lower_depth))
        behind = jnp.where(flipped, lower_seen, upper_seen)
        brick_depth = ex_ref[ch, 0, 0:1]
        front, brick_grad = to_samples(
            through_front, -through_front * jnp.exp(-brick_depth) * behind
        )
        lg_ref[mine, :] = (front * q_ref[mine, :] + brick_grad) * len_ref[mine, :]
        c_ref[mine, :] = front * c_ref[mine, :]

    def feature_grads(p):
        left, right = [], []
        for k in range(2):
            t = 2 * p + k
            c_hi, c_low = split_two(c_ref[pl.ds(t, 1), :] * group_mask)
            lgm = lg_ref[pl.ds(t, 1), :] * group_mask
            s_hi, s_low = split_two(sc_ref[pl.ds(t * group, group), :])
            left += [c_hi, c_hi, c_low, lgm]
            right += [side(s_hi, k), side(s_low, k), side(s_hi, k), side(unit, k)]
        left = jnp.concatenate(left, axis=0).astype(BF16)
        right = jnp.concatenate(right, axis=0).astype(BF16)
        fg = contract_rows(left, right).astype(BF16)
        put_pair(p1_ref, p, fg)

    def ray_sums(p):
        sums = []
        for k in range(2):
            t = 2 * p + k
            c_hi, c_low = split_two(c_ref[pl.ds(t, 1), :] * group_mask)
            sums += [c_hi, c_low, lg_ref[pl.ds(t, 1), :] * group_mask]
        sums = jnp.concatenate(sums, axis=0).astype(BF16)
        got = jnp.dot(sums, pair_of(h2_ref, p), preferred_element_type=F32)
        dens = jnp.zeros((group, width), F32)
        for k in range(2):
            base = 3 * group * k
            mine = got[:, k * width : (k + 1) * width]
            u_ref[pl.ds((2 * p + k) * group, group), :] = (
                mine[base : base + group] + mine[base + group : base + 2 * group]
            )
            dens = dens + mine[base + 2 * group : base + 3 * group]
        return dens

    def back_two(p):
        h2g = jnp.dot(pair_of(p1_ref, p), wfb[...], preferred_element_type=F32)
        put_pair(p2_ref, p, (h2g * s2_ref[p]).astype(BF16))

    def back_one(p):
        h1g = jnp.dot(pair_of(p2_ref, p), w2b[...], preferred_element_type=F32)
        put_pair(p1_ref, p, (h1g * slope_of(s1_ref, f1_ref, p)).astype(BF16))

    def finish(p):
        got = jnp.dot(pair_of(p1_ref, p), w1b[...], preferred_element_type=F32).astype(BF16)
        o_ref[pl.ds(p * span, LANES), :] = got[:, :width]
        o_ref[pl.ds(p * span + LANES, LANES), :] = got[:, width:]

    def weight_grad(turned, grads, ch):
        total = None
        for t0 in range(ch * tiles_c, (ch + 1) * tiles_c, K_TILES):
            left = jnp.concatenate(
                [turned[t] for t in range(t0, t0 + K_TILES)], axis=1
            )
            right = grads[pl.ds(t0, K_TILES)].reshape(K_TILES * LANES, width)
            got = jnp.dot(left, right, preferred_element_type=F32)
            total = got if total is None else total + got
        return total

    share = width // n_ray

    def red_copy(d, m):
        to = lax.rem(my_ray + d, n_ray)
        return pltpu.make_async_remote_copy(
            src_ref=acc.at[pl.ds(m, 1), pl.ds(pl.multiple_of(to * share, share), share), :],
            dst_ref=red_ref.at[d, pl.ds(m, 1)],
            send_sem=red_send.at[m * n_ray + d],
            recv_sem=red_recv.at[m * n_ray + d],
            device_id={"ray": to},
            device_id_type=MESH,
        )

    partners = sorted(range(1, n_ray), key=lambda d: abs(d - n_ray // 2))

    def add_grad(m, value, ch):
        acc[m] = value if ch == 0 else acc[m] + value

    def late_layers(ch):
        first, last = ch * pairs_c, (ch + 1) * pairs_c
        for p in range(first, last + 2, 2):
            for k in (p, p + 1):
                if k < last:
                    second_layer(k)
            for k in (p - 2, p - 1):
                if k >= first:
                    heads(k)

    for p in range(EARLY_PAIRS):
        first_layer(p)
    pieces[1].wait()
    for p in range(EARLY_PAIRS, pairs_c):
        first_layer(p)
    late_layers(0)
    for ch in range(1, CHUNKS):
        first = ch * pairs_c
        pieces[ch + 1].wait()
        middle(ch - 1)
        for p in range(first, first + HEAD_START):
            first_layer(p)
        send(ch - 1)
        for p in range(first + HEAD_START, first + pairs_c):
            first_layer(p)
        late_layers(ch)
    middle(CHUNKS - 1)
    send(CHUNKS - 1)
    for p in range(pairs):
        turn(p)

    dens = jnp.zeros((group, width), F32)
    for ch in range(CHUNKS):
        first, last = ch * pairs_c, (ch + 1) * pairs_c
        composite(ch)
        if ch > 0:
            add_grad(0, weight_grad(xt_ref, p1_ref, ch - 1), ch - 1)
        for p in range(first, last):
            feature_grads(p)
        for p in range(first, last):
            dens = dens + ray_sums(p)
        for p in range(first, last):
            back_two(p)
        if ch < CHUNKS - 1:
            for p in range(first, last):
                back_one(p)
            add_grad(1, weight_grad(h1t_ref, p2_ref, ch), ch)
    u_hi, u_low = split_two(u_ref[...])
    s_hi, s_low = split_two(sc_ref[...])
    left = jnp.concatenate([u_hi, u_hi, u_low, *split_three(dens)], axis=0)
    right = jnp.concatenate([s_hi, s_low, s_hi, unit, unit, unit], axis=0)
    acc[2] = contract_rows(left.astype(BF16), right.astype(BF16))
    add_grad(1, weight_grad(h1t_ref, p2_ref, CHUNKS - 1), CHUNKS - 1)
    for d in partners:
        red_copy(d, 1).start()
        red_copy(d, 2).start()
    for p in range(pairs - pairs_c, pairs):
        back_one(p)
    add_grad(0, weight_grad(xt_ref, p1_ref, CHUNKS - 1), CHUNKS - 1)
    for d in partners:
        red_copy(d, 0).start()
    for p in range(pairs):
        finish(p)

    def reduced(m):
        total = acc[m, pl.ds(pl.multiple_of(my_ray * share, share), share), :]
        for d in partners:
            red_copy(d, m).wait()
            total = total + red_ref[d, m]
        return total * (1.0 / LOSS_SCALE)

    both = reduced(2)
    g3_ref[0] = both[:, :feat]
    g4_ref[...] = both.T[feat : feat + 1, :]
    g2_ref[0] = reduced(1)
    g1_ref[0] = reduced(0)


def hand_out(*refs):
    held, out, sems = refs[:5], refs[5:10], refs[10]
    copies = [pltpu.make_async_copy(held[i], out[i], sems.at[i]) for i in range(5)]
    for copy in copies:
        copy.start()
    for copy in copies:
        copy.wait()


def solution(mesh):
    n_brick, n_ray = mesh.shape["brick"], mesh.shape["ray"]

    def shards(samples_in, sample_count, step_length, view_flip, pixel_grad, w1, w2, wf, wd):
        rays, _, per_ray, width = samples_in.shape
        feat = pixel_grad.shape[0]
        rows = rays * per_ray
        pairs = rows // (2 * LANES)
        tiles = rows // LANES
        share = width // n_ray
        vmem = pl.BlockSpec(memory_space=pltpu.VMEM)
        hbm = pl.BlockSpec(memory_space=pl.ANY)
        tile_shape = (tiles, LANES, width)
        turned_shape = (tiles, width, LANES)
        outs = pl.pallas_call(
            functools.partial(kernel, n_brick, n_ray, per_ray),
            out_shape=(
                pltpu.VMEM((rows, width), BF16),
                pltpu.VMEM((1, share, width), F32),
                pltpu.VMEM((1, share, width), F32),
                pltpu.VMEM((1, share, feat), F32),
                pltpu.VMEM((1, share), F32),
            ),
            in_specs=[hbm] * 9,
            out_specs=(vmem,) * 5,
            scratch_shapes=[
                pltpu.VMEM((rows, width), BF16),
                pltpu.VMEM((1, rays), jnp.int32),
                pltpu.VMEM((1, rays), F32),
                pltpu.VMEM((1, rays), jnp.int32),
                pltpu.VMEM((feat, rays), F32),
                pltpu.VMEM((1, width, width), BF16),
                pltpu.VMEM((1, width, width), BF16),
                pltpu.VMEM((1, feat, width), BF16),
                pltpu.VMEM((1, width), BF16),
                pltpu.VMEM(turned_shape, BF16),
                pltpu.VMEM(tile_shape, BF16),
                pltpu.VMEM(turned_shape, BF16),
                pltpu.VMEM(tile_shape, BF16),
                pltpu.VMEM(tile_shape, BF16),
                pltpu.VMEM(tile_shape, BF16),
                pltpu.VMEM((pairs, LANES, 2 * width), F32),
                pltpu.VMEM((pairs, LANES, 2 * width), F32),
                pltpu.VMEM((pairs, LANES, 2 * width), F32),
                pltpu.VMEM((rays, width), F32),
                pltpu.VMEM((rays, width), F32),
                pltpu.VMEM((tiles, LANES), F32),
                pltpu.VMEM((tiles, LANES), F32),
                pltpu.VMEM((tiles, LANES), F32),
                pltpu.VMEM((tiles, LANES), F32),
                pltpu.VMEM((rays, width), F32),
                pltpu.VMEM((2 * width, 2 * width), BF16),
                pltpu.VMEM((2 * width, 2 * width), BF16),
                pltpu.VMEM((2 * width, 2 * width), BF16),
                pltpu.VMEM((2 * width, 2 * width), BF16),
                pltpu.VMEM((2 * width, 2 * width), BF16),
                pltpu.VMEM((3, width, width), F32),
                pltpu.VMEM((CHUNKS, n_brick, 8, rays // CHUNKS), F32),
                pltpu.VMEM((n_ray, 3, share, width), F32),
                pltpu.SemaphoreType.DMA((8,)),
                pltpu.SemaphoreType.DMA((CHUNKS + 1,)),
                pltpu.SemaphoreType.DMA((CHUNKS, n_brick)),
                pltpu.SemaphoreType.DMA((CHUNKS, n_brick)),
                pltpu.SemaphoreType.DMA((3 * n_ray,)),
                pltpu.SemaphoreType.DMA((3 * n_ray,)),
            ],
            compiler_params=pltpu.CompilerParams(
                collective_id=0, has_side_effects=True, vmem_limit_bytes=52 * 1024 * 1024
            ),
        )(
            samples_in.reshape(rows, width),
            sample_count.reshape(1, rays),
            step_length.reshape(1, rays),
            view_flip.reshape(1, rays),
            pixel_grad,
            w1,
            w2,
            jnp.swapaxes(wf, 1, 2),
            wd,
        )
        outs = pl.pallas_call(
            hand_out,
            out_shape=tuple(jax.ShapeDtypeStruct(o.shape, o.dtype) for o in outs),
            in_specs=[vmem] * 5,
            out_specs=(hbm,) * 5,
            scratch_shapes=[pltpu.SemaphoreType.DMA((5,))],
            compiler_params=pltpu.CompilerParams(vmem_limit_bytes=4 * 1024 * 1024),
        )(*[pltpu.with_memory_space_constraint(o, pltpu.VMEM) for o in outs])
        return (outs[0].reshape(samples_in.shape),) + tuple(outs[1:])

    placed = (
        P(("groups", "ray"), "brick", None, None),
        P(("groups", "ray"), "brick"),
        P(("groups", "ray")),
        P(("groups", "ray")),
        P(None, ("groups", "ray")),
        P("brick", None, None),
        P("brick", None, None),
        P("brick", None, None),
        P("brick", None),
    )
    return jax.shard_map(
        shards,
        mesh=mesh,
        in_specs=placed,
        out_specs=(
            P(("groups", "ray"), "brick", None, None),
            P(("groups", "brick"), "ray", None),
            P(("groups", "brick"), "ray", None),
            P(("groups", "brick"), "ray", None),
            P(("groups", "brick"), "ray"),
        ),
        check_vma=False,
    )
```
